256 devices in a mesh: row: 32 (over y, z), col: 8 (over x, core).
Axes of the slice: x: 4, y: 4, z: 8, core: 2. Of those that a mesh axis runs over, the one named last changes fastest.
Arguments:
- tokens: bfloat16 [1536, 8192], P('row', 'col'), may hold values from -6 to 6
- weight: bfloat16 [8192, 32768], P('col', 'row'), may hold values from -0.109375 to 0.109375
- tile_rows: int32 [32, 8, 32], P('row', 'col'), may hold values from 0 to 63, as said below
- tile_cols: int32 [32, 8, 32], P('row', 'col'), may hold values from 0 to 255, as said below
- tile_count: int32 [32, 8], P('row', 'col'), may hold values from 8 to 32, as said below
- hidden_cotangent: bfloat16 [1536, 32768], P('col', 'row'), may hold values from -6 to 6
Outputs:
- hidden: bfloat16 [1536, 32768], P('col', 'row')
- input_grad: bfloat16 [1536, 8192], P('row', 'col')
- weight_grad: bfloat16 [8192, 32768], P('col', 'row')
The draws below stay inside these ranges and needn't reach their ends.
Inputs may be any that keep to these rules, and one draw needn't show every extreme that they name: tile_rows[r, c, k] is a row block of the weight (tiles of 128 x 128) among the 8 blocks from c * 8 on, which index c of col holds. tile_cols[r, c, k] is a column block among the 8 blocks from r * 8 on, which index r of row holds; the 32 candidate tiles of one device are distinct. The first tile_count[r, c] candidates of device (r, c) are its nonzero tiles; some device holds 32.
All inputs are finite; a program needn't handle non-finite values.
Results may differ from the reference program's by a relative error of at most 0.0049.
Values may be sent and summed in bfloat16 or wider, within the bound.
No kernel may reach another device: no remote copies, remote signals or barrier semaphores. Data moves between devices by JAX's collectives and lax.ppermute only.
A program may use at most 128 MiB of HBM per device.

```python
import jax
import jax.numpy as jnp

D = 8192
FF = 32768
TILE = 128
TOKENS = 1536
RBD = 8
CBD = 8
BLOCKS_DEV = 64
CAP = 32
N_ROW = 32
N_COL = 8


def tile_slots(key):
    scores = jax.random.randint(jax.random.fold_in(key, 7), (N_ROW, N_COL, BLOCKS_DEV), 0, 2 ** 20)
    scores = scores * BLOCKS_DEV + jnp.arange(BLOCKS_DEV, dtype=jnp.int32)
    ordering = jnp.argsort(scores, axis=-1, stable=True)
    return ordering[:, :, :CAP].astype(jnp.int32)


def draw_tile_rows(key, part):
    slots = tile_slots(key)
    offset = (jnp.arange(N_COL, dtype=jnp.int32) * RBD)[None, :, None]
    return (offset + slots // CBD).astype(jnp.int32)


def draw_tile_cols(key, part):
    slots = tile_slots(key)
    offset = (jnp.arange(N_ROW, dtype=jnp.int32) * CBD)[:, None, None]
    return (offset + slots % CBD).astype(jnp.int32)


def draw_tile_count(key, part):
    counts = jax.random.randint(jax.random.fold_in(key, 11), (N_ROW, N_COL), CAP // 4, CAP + 1)
    chosen = jax.random.randint(jax.random.fold_in(key, 13), (), 0, N_ROW * N_COL)
    flat_index = jnp.arange(N_ROW * N_COL, dtype=jnp.int32).reshape(N_ROW, N_COL)
    return jnp.where(flat_index == chosen, CAP, counts).astype(jnp.int32)


def steps_of(key, dims, cuts, least, high):
    level = 1.0
    for dim, blocks in cuts:
        steps = jax.random.uniform(jax.random.fold_in(jax.random.fold_in(key, 6), dim), (blocks,), jnp.float32, least / len(cuts), high / len(cuts))
        level = level * jnp.repeat(jnp.exp(steps), dims[dim] // blocks).reshape((-1,) + (1,) * (len(dims) - 1 - dim))
    return level


def noise(rng, dims, width, limit, split=(), kind=jnp.bfloat16):
    array = jax.random.normal(rng, dims, jnp.float32) * width
    if len(split) > 0:
        array = steps_of(rng, dims, split, -0.22, 0.18) * array
    return jnp.clip(array, min=-limit, max=limit).astype(kind)


def setup_inputs(seed: int = 0) -> dict:
    keys = jax.random.split(jax.random.key(seed), 7)
    tokens = noise(keys[0], (TOKENS, D), 1.0, 6.0, ((0, 32), (1, 8)))
    weight = noise(keys[1], (D, FF), (D // 3) ** -0.5, 0.109375, ((0, 8), (1, 32)))
    tile_rows = draw_tile_rows(jax.random.fold_in(keys[6], 71), 0)
    tile_cols = draw_tile_cols(jax.random.fold_in(keys[6], 71), 0)
    tile_count = draw_tile_count(jax.random.fold_in(keys[6], 71), 0)
    hidden_cotangent = noise(keys[5], (TOKENS, FF), 1.0, 6.0, ((0, 8), (1, 32)))
    return dict(tokens=tokens, weight=weight, tile_rows=tile_rows, tile_cols=tile_cols, tile_count=tile_count, hidden_cotangent=hidden_cotangent)


def reference(tokens, weight, tile_rows, tile_cols, tile_count, hidden_cotangent):
    row_list = tile_rows.reshape(-1).astype(jnp.int32)
    col_list = tile_cols.reshape(-1).astype(jnp.int32)
    is_live = (jnp.arange(CAP)[None, :] < tile_count.reshape(-1, 1)).reshape(-1).astype(jnp.float32)
    block_mask = jnp.zeros((D // TILE, FF // TILE), jnp.float32).at[row_list, col_list].max(is_live)
    dense_mask = jnp.repeat(jnp.repeat(block_mask.astype(jnp.bfloat16), TILE, 0), TILE, 1)
    masked = weight * dense_mask
    pre_act = jnp.dot(tokens, masked, preferred_element_type=jnp.float32)
    gate_value = jax.nn.sigmoid(pre_act)
    hidden = (pre_act * gate_value).astype(jnp.bfloat16)
    silu_slope = gate_value * (1.0 + pre_act * (1.0 - gate_value))
    grad_pre = (hidden_cotangent.astype(jnp.float32) * silu_slope).astype(jnp.bfloat16)
    input_grad = jnp.dot(grad_pre, masked.T, preferred_element_type=jnp.float32).astype(jnp.bfloat16)
    full_grad = jnp.dot(tokens.T, grad_pre, preferred_element_type=jnp.float32)
    weight_grad = jnp.where(dense_mask > 0, full_grad, jnp.zeros_like(full_grad)).astype(jnp.bfloat16)
    return hidden, input_grad, weight_grad
```

```python
import jax
import jax.numpy as jnp
from jax import lax
from jax.experimental import pallas as pl
from jax.experimental.pallas import tpu as pltpu
from jax.sharding import Mesh
from jax.sharding import PartitionSpec as P

TILE = 128
SIZES = {"y": 4, "z": 8, "x": 4, "core": 2}
ROW = ("y", "z")
COL = ("x", "core")
VM = pltpu.VMEM
F32 = jnp.float32
BF16 = jnp.bfloat16


def from_ahead(value, axis, k):
    n = SIZES[axis]
    return lax.ppermute(value, axis, [((i + k) % n, i) for i in range(n)])


def to_ahead(value, axis, k):
    n = SIZES[axis]
    return lax.ppermute(value, axis, [(i, (i + k) % n) for i in range(n)])


def call(body, outs, smem, vmem, flops=0, scratch=(), limit=40):
    outs = [jax.ShapeDtypeStruct(s, d) for s, d in outs]
    return pl.pallas_call(
        body,
        out_shape=outs,
        in_specs=[pl.BlockSpec(memory_space=pltpu.SMEM)] * len(smem)
        + [pl.BlockSpec(memory_space=VM)] * len(vmem),
        out_specs=[pl.BlockSpec(memory_space=VM)] * len(outs),
        scratch_shapes=list(scratch),
        compiler_params=pltpu.CompilerParams(vmem_limit_bytes=limit * 2**20),
        cost_estimate=pl.CostEstimate(
            flops=flops,
            transcendentals=0,
            bytes_accessed=sum(v.size * v.dtype.itemsize for v in vmem)
            + sum(o.size * o.dtype.itemsize for o in outs),
        ),
    )(*smem, *vmem)


def tile_ref(ref, r, c):
    return ref.at[
        pl.ds(pl.multiple_of(r * TILE, TILE), TILE), pl.ds(pl.multiple_of(c * TILE, TILE), TILE)
    ]


def mask_body(rows, cols, count, w, out, flipped):
    out[...] = jnp.zeros_like(out)
    flipped[...] = jnp.zeros_like(flipped)

    @pl.loop(0, count[0])
    def _(k):
        tile = tile_ref(w, rows[k], cols[k])[...]
        tile_ref(out, rows[k], cols[k])[...] = tile
        tile_ref(flipped, cols[k], rows[k])[...] = tile.T


def place_body(pos, *refs):
    pieces, out = refs[:-1], refs[-1]
    for i, piece in enumerate(pieces):
        out[(pos[1] + i) % SIZES["z"]] = piece[...]


def up_body(pos, tok, w, keep, send, acc):
    core = pos[3]
    rows = keep.shape[0]
    part = jnp.dot(tok[...].reshape(2 * rows, tok.shape[2]), w[...], preferred_element_type=F32)
    acc[...] = part.reshape(acc.shape)
    keep[...] = acc[core]
    send[...] = acc[1 - core].astype(BF16)


def add_body(pos, *refs):
    keep, recv, out = refs[:4], refs[4:8], refs[8:]
    shift = pos[2] - pos[0] + 4
    for d in range(4):
        for j in range(4):

            @pl.when((shift + d) % 4 == j)
            def _(d=d, j=j):
                @pl.loop(0, out[d].shape[0] // 16)
                def _(i):
                    at = pl.ds(pl.multiple_of(i * 16, 16), 16)
                    total = keep[j][at] + recv[j][at].astype(F32)
                    out[d][at] = total.astype(out[d].dtype)


def fetch(choice, pieces, slots, sems):
    def each(act):
        for i in range(4):
            for k in range(4):

                @pl.when(choice(i) == k)
                def _(i=i, k=k):
                    act(pltpu.make_async_copy(pieces[k], slots(i), sems.at[i]))

    each(lambda c: c.start())
    return lambda: each(lambda c: c.wait())


def back_body(pos, *refs):
    mine, other, w, out = refs[:4], refs[4:8], refs[8], refs[9:13]
    grads, sems = refs[13:]
    core = pos[3]
    shift = pos[0] - pos[2] + 4
    waits = [
        fetch(lambda j: (shift + j) % 4, g, lambda j, s=s: grads.at[j, s], sems.at[k])
        for k, (s, g) in enumerate(((core, mine), (1 - core, other)))
    ]
    for wait in waits:
        wait()

    for j in range(4):
        part = jnp.dot(
            grads[j].reshape(-1, w.shape[0]), w[...], preferred_element_type=F32
        )
        out[j][...] = part.astype(out[j].dtype).reshape(out[j].shape)


def sum_y_body(pos, own, r1, r2, r3, *out):
    n = SIZES["z"]
    for i in range(n):
        b = (pos[1] + i) % n
        total = own[b] + r1[b].astype(F32) + r2[b].astype(F32) + r3[b].astype(F32)
        out[i][...] = total.astype(out[i].dtype)


def wgrad_body(pos, rows, cols, count, *refs):
    out, toks, grads, acc, sems = refs[-5:]
    refs = refs[:-5]
    n = len(refs) // 12
    core = pos[3]
    shift = pos[2] - pos[0] + 4
    waits = []
    for k in range(n):
        tok, mine, other = (refs[12 * k + 4 * s : 12 * k + 4 * s + 4] for s in range(3))
        moves = (
            (tok, lambda d: (shift + d) % 4, lambda d, k=k: toks.at[k, d]),
            (mine, lambda d: d, lambda d, k=k: grads.at[k, d, core]),
            (other, lambda d: d, lambda d, k=k: grads.at[k, d, 1 - core]),
        )
        for m, (pieces, choice, slots) in enumerate(moves):
            waits.append(fetch(choice, pieces, slots, sems.at[k, m]))
    acc[...] = jnp.zeros_like(acc)
    for wait in waits:
        wait()
    for k in range(n):

        @pl.loop(0, 4)
        def _(d, k=k):
            t = toks[k, d].reshape(-1, toks.shape[-1])
            g = grads[k, d].reshape(-1, grads.shape[-1])
            acc[...] += lax.dot_general(
                t, g, (((0,), (0,)), ((), ())), preferred_element_type=F32
            )

    out[...] = jnp.zeros_like(out)

    @pl.loop(0, count[0])
    def _(k):
        tile_ref(out, rows[k], cols[k])[...] = tile_ref(acc, rows[k], cols[k])[...].astype(BF16)


def gather_tokens(part, pos):
    rows, width = part.shape
    zs = [part] + [from_ahead(part, "z", i) for i in range(1, 8)]
    (own,) = call(place_body, [((8, rows, width), BF16)], [pos], zs)
    return [own] + [from_ahead(own, "y", j) for j in range(1, 4)]


def forward(blocks, wm, pos, cot):
    rows = blocks[0].shape[1] * 4
    depth, width = wm.shape
    keeps, recvs = [], []
    for block in blocks:
        keep, send = call(
            up_body,
            [((rows, width), F32), ((rows, width), BF16)],
            [pos],
            [block, wm],
            4 * rows * depth * width,
            [VM((2, rows, width), F32)],
        )
        keeps.append(keep)
        recvs.append(to_ahead(send, "core", 1))
    shape = (rows, width)
    own, *sends = call(add_body, [(shape, F32)] + [(shape, BF16)] * 3, [pos], keeps + recvs)
    pre_act = own
    for d, send in enumerate(sends):
        pre_act = pre_act + to_ahead(send, "x", d + 1).astype(F32)
    gate = jax.nn.sigmoid(pre_act)
    hidden = (pre_act * gate).astype(BF16)
    slope = gate * (1.0 + pre_act * (1.0 - gate))
    grad_pre = (cot.astype(F32) * slope).astype(BF16)
    return hidden, grad_pre


def gather_grads(grad_pre):
    mine = [grad_pre] + [from_ahead(grad_pre, "x", d) for d in range(1, 4)]
    other = [to_ahead(g, "core", 1) for g in mine]
    return mine, other


def backward(mine, other, flipped, pos):
    rows = mine[0].shape[0] // 4
    width, depth = flipped.shape
    shape = (8, rows, depth)
    own, *sends = call(
        back_body,
        [(shape, F32)] + [(shape, BF16)] * 3,
        [pos],
        mine + other + [flipped],
        64 * rows * depth * width,
        [VM((4, 2, 4 * rows, width), BF16), pltpu.SemaphoreType.DMA((2, 4))],
    )
    recvs = [to_ahead(s, "y", j + 1) for j, s in enumerate(sends)]
    shape = (rows, depth)
    own, *sends = call(sum_y_body, [(shape, F32)] + [(shape, BF16)] * 7, [pos], [own] + recvs)
    total = own
    for i, s in enumerate(sends):
        total = total + to_ahead(s, "z", i + 1).astype(F32)
    return total.astype(BF16)


CUTS = ((0, 48),)


def on_device(tokens, weight, tile_rows, tile_cols, tile_count, hidden_cotangent):
    y, z, x, core = (lax.axis_index(a) for a in ("y", "z", "x", "core"))
    pos = jnp.stack([y, z, x, core]).astype(jnp.int32)
    row_blocks = weight.shape[0] // TILE
    col_blocks = weight.shape[1] // TILE
    rows = tile_rows.reshape(-1) - (x * 2 + core) * row_blocks
    cols = tile_cols.reshape(-1) - (y * 8 + z) * col_blocks
    count = tile_count.reshape(1)
    wm, flipped = call(mask_body, [(weight.shape, BF16), (weight.shape[::-1], BF16)], [rows, cols, count], [weight])
    cot4 = hidden_cotangent.reshape(4, 48, -1)
    hiddens, in_grads, saved = [], [], []
    for a, b in CUTS:
        blocks = gather_tokens(tokens[a:b], pos)
        cot = cot4[:, a:b].reshape((b - a) * 4, -1)
        hidden, grad_pre = forward(blocks, wm, pos, cot)
        mine, other = gather_grads(grad_pre)
        in_grads.append(backward(mine, other, flipped, pos))
        hiddens.append(hidden.reshape(4, b - a, -1))
        saved += blocks + mine + other
    n, per = len(CUTS), (CUTS[0][1] - CUTS[0][0]) * 4
    (weight_grad,) = call(
        wgrad_body,
        [(weight.shape, BF16)],
        [pos, rows, cols, count],
        saved,
        2 * 1536 * weight.size,
        [
            VM((n, 4, 8, per // 4, weight.shape[0]), BF16),
            VM((n, 4, 2, per, weight.shape[1]), BF16),
            VM(weight.shape, F32),
            pltpu.SemaphoreType.DMA((n, 3, 4)),
        ],
    )
    hidden = jnp.concatenate(hiddens, axis=1).reshape(192, -1)
    return hidden, jnp.concatenate(in_grads, axis=0), weight_grad


def solution(mesh):
    split = Mesh(mesh.devices.reshape(4, 8, 4, 2), ("y", "z", "x", "core"))
    return jax.shard_map(
        on_device,
        mesh=split,
        in_specs=(
            P(ROW, COL),
            P(COL, ROW),
            P(ROW, COL, None),
            P(ROW, COL, None),
            P(ROW, COL),
            P(COL, ROW),
        ),
        out_specs=(P(COL, ROW), P(ROW, COL), P(COL, ROW)),
        check_vma=False,
    )
```

```python
import jax
import jax.numpy as jnp
from jax import lax
from jax.experimental import pallas as pl
from jax.experimental.pallas import tpu as pltpu
from jax.sharding import Mesh
from jax.sharding import PartitionSpec as P

TILE = 128
SIZES = {"y": 4, "z": 8, "x": 4, "core": 2}
ROW = ("y", "z")
COL = ("x", "core")
VM = pltpu.VMEM
F32 = jnp.float32
BF16 = jnp.bfloat16
STEPS = (0, 1, 2, -1)


def from_ahead(value, axis, k):
    n = SIZES[axis]
    return lax.ppermute(value, axis, [((i + k) % n, i) for i in range(n)])


def to_ahead(value, axis, k):
    n = SIZES[axis]
    return lax.ppermute(value, axis, [(i, (i + k) % n) for i in range(n)])


def call(body, outs, smem, vmem, flops=0, scratch=(), limit=40):
    outs = [jax.ShapeDtypeStruct(s, d) for s, d in outs]
    return pl.pallas_call(
        body,
        out_shape=outs,
        in_specs=[pl.BlockSpec(memory_space=pltpu.SMEM)] * len(smem)
        + [pl.BlockSpec(memory_space=VM)] * len(vmem),
        out_specs=[pl.BlockSpec(memory_space=VM)] * len(outs),
        scratch_shapes=list(scratch),
        compiler_params=pltpu.CompilerParams(vmem_limit_bytes=limit * 2**20),
        cost_estimate=pl.CostEstimate(
            flops=flops,
            transcendentals=0,
            bytes_accessed=sum(v.size * v.dtype.itemsize for v in vmem)
            + sum(o.size * o.dtype.itemsize for o in outs),
        ),
    )(*smem, *vmem)


def tile_ref(ref, r, c):
    return ref.at[
        pl.ds(pl.multiple_of(r * TILE, TILE), TILE), pl.ds(pl.multiple_of(c * TILE, TILE), TILE)
    ]


def mask_body(rows, cols, count, w, out, flipped):
    out[...] = jnp.zeros_like(out)
    flipped[...] = jnp.zeros_like(flipped)

    @pl.loop(0, count[0])
    def _(k):
        tile = tile_ref(w, rows[k], cols[k])[...]
        tile_ref(out, rows[k], cols[k])[...] = tile
        tile_ref(flipped, cols[k], rows[k])[...] = tile.T


def zpos(pos, i, hi):
    return (pos[1] + i + 4 * hi + 8) % 8


def up_body(pos, *refs):
    a3, b3, w = refs[:4], refs[4:8], refs[8]
    keep, send, toks, acc = refs[9:]
    core = pos[3]
    cut = a3[0].shape[-1]
    rows = keep.shape[1]
    back = pos[0] - pos[2] + 4
    for j in range(4):
        d = (j + back) % 4
        for i in range(4):
            for hi in range(2):
                at = zpos(pos, STEPS[i], hi)
                toks[d, at, :, :cut] = a3[i][j, hi]
                toks[d, at, :, cut:] = b3[j][i, hi]

    @pl.loop(0, 4)
    def _(d):
        part = jnp.dot(
            toks[d].reshape(2 * rows, toks.shape[-1]), w[...], preferred_element_type=F32
        )
        acc[...] = part.reshape(acc.shape)
        keep[d] = acc[core]
        send[d] = acc[1 - core].astype(BF16)


def back_body(pos, *refs):
    mine, other, w = refs[:4], refs[4:8], refs[8]
    a3, b3, grads = refs[9:13], refs[13:17], refs[17]
    acc, sems = refs[18:]
    core = pos[3]
    cut = a3[0].shape[-1]
    back = pos[0] - pos[2] + 4
    copies = [
        pltpu.make_async_copy(g[d], grads.at[d, side], sems.at[s, d])
        for s, (side, g) in enumerate(((core, mine), (1 - core, other)))
        for d in range(4)
    ]
    for c in copies:
        c.start()
    for c in copies:
        c.wait()
    for j in range(4):
        part = jnp.dot(
            grads[(j + back) % 4].reshape(-1, w.shape[0]), w[...], preferred_element_type=F32
        )
        acc[...] = part.reshape(acc.shape)
        for i in range(4):
            for hi in range(2):
                piece = acc[zpos(pos, STEPS[i], hi)]
                a3[i][j, hi] = piece[:, :cut].astype(a3[i].dtype)
                b3[j][i, hi] = piece[:, cut:].astype(b3[j].dtype)


def wgrad_body(rows, cols, count, toks, grads, out, acc):
    acc[...] = jnp.zeros_like(acc)

    @pl.loop(0, 4)
    def _(d):
        t = toks[d].reshape(-1, toks.shape[-1])
        g = grads[d].reshape(-1, grads.shape[-1])
        acc[...] += lax.dot_general(t, g, (((0,), (0,)), ((), ())), preferred_element_type=F32)

    out[...] = jnp.zeros_like(out)

    @pl.loop(0, count[0])
    def _(k):
        tile_ref(out, rows[k], cols[k])[...] = tile_ref(acc, rows[k], cols[k])[...].astype(BF16)


def gather_four(piece, axis):
    return [piece] + [from_ahead(piece, axis, k) for k in STEPS[1:]]


def gather_tokens(tokens):
    pair = jnp.stack([tokens, from_ahead(tokens, "z", 4)])
    cut = tokens.shape[1] // 2
    a2 = jnp.stack(gather_four(pair[:, :, :cut], "y"))
    b2 = jnp.stack(gather_four(pair[:, :, cut:], "z"))
    return gather_four(a2, "z"), gather_four(b2, "y")


def forward(a3, b3, wm, pos, cot):
    rows = a3[0].shape[2] * 4
    depth, width = wm.shape
    keep, send, toks = call(
        up_body,
        [
            ((4, rows, width), F32),
            ((4, rows, width), BF16),
            ((4, 8, rows // 4, depth), BF16),
        ],
        [pos],
        a3 + b3 + [wm],
        16 * rows * depth * width,
        [VM((2, rows, width), F32)],
    )
    total = keep + to_ahead(send, "core", 1).astype(F32)
    pre_act = total[0]
    for d in range(1, 4):
        pre_act = pre_act + to_ahead(total[d].astype(BF16), "x", d).astype(F32)
    gate = jax.nn.sigmoid(pre_act)
    hidden = (pre_act * gate).astype(BF16)
    slope = gate * (1.0 + pre_act * (1.0 - gate))
    grad_pre = (cot.astype(F32) * slope).astype(BF16)
    return hidden, grad_pre, toks


def gather_grads(grad_pre):
    mine = [grad_pre] + [from_ahead(grad_pre, "x", d) for d in range(1, 4)]
    other = [to_ahead(g, "core", 1) for g in mine]
    return mine, other


def reduce_four(own, sends, axis):
    total = own
    for k, s in zip(STEPS[1:], sends):
        total = total + to_ahead(s.astype(BF16), axis, k).astype(F32)
    return total


def backward(mine, other, flipped, pos, finish):
    rows = mine[0].shape[0]
    width, depth = flipped.shape
    shape = (4, 2, rows // 4, depth // 2)
    outs = [(shape, F32)] + [(shape, BF16)] * 3
    *parts, grads = call(
        back_body,
        outs + outs + [((4, 2, rows, width), BF16)],
        [pos],
        mine + other + [flipped],
        16 * rows * depth * width,
        [VM((8, rows // 4, depth), F32), pltpu.SemaphoreType.DMA((2, 4))],
    )
    weight_grad = finish(grads)
    a2 = reduce_four(parts[0], parts[1:4], "z")
    b2 = reduce_four(parts[4], parts[5:], "y")
    a2, b2, weight_grad = lax.optimization_barrier((a2, b2, weight_grad))
    a1 = reduce_four(a2[0], a2[1:], "y")
    b1 = reduce_four(b2[0], b2[1:], "z")
    both = jnp.concatenate([a1, b1], axis=-1)
    total = both[0] + to_ahead(both[1].astype(BF16), "z", 4).astype(F32)
    return total.astype(BF16), weight_grad


def on_device(tokens, weight, tile_rows, tile_cols, tile_count, hidden_cotangent):
    y, z, x, core = (lax.axis_index(a) for a in ("y", "z", "x", "core"))
    pos = jnp.stack([y, z, x, core]).astype(jnp.int32)
    row_blocks = weight.shape[0] // TILE
    col_blocks = weight.shape[1] // TILE
    rows = tile_rows.reshape(-1) - (x * 2 + core) * row_blocks
    cols = tile_cols.reshape(-1) - (y * 8 + z) * col_blocks
    count = tile_count.reshape(1)
    shapes = [(weight.shape, BF16), (weight.shape[::-1], BF16)]
    wm, flipped = call(mask_body, shapes, [rows, cols, count], [weight])
    a3, b3 = gather_tokens(tokens)
    hidden, grad_pre, toks = forward(a3, b3, wm, pos, hidden_cotangent)
    mine, other = gather_grads(grad_pre)

    def finish(grads):
        (weight_grad,) = call(
            wgrad_body,
            [(weight.shape, BF16)],
            [rows, cols, count],
            [toks, grads],
            2 * 1536 * weight.size,
            [VM(weight.shape, F32)],
        )
        return weight_grad

    input_grad, weight_grad = backward(mine, other, flipped, pos, finish)
    return hidden, input_grad, weight_grad


def solution(mesh):
    split = Mesh(mesh.devices.reshape(4, 8, 4, 2), ("y", "z", "x", "core"))
    return jax.shard_map(
        on_device,
        mesh=split,
        in_specs=(
            P(ROW, COL),
            P(COL, ROW),
            P(ROW, COL, None),
            P(ROW, COL, None),
            P(ROW, COL),
            P(COL, ROW),
        ),
        out_specs=(P(COL, ROW), P(ROW, COL), P(COL, ROW)),
        check_vma=False,
    )
```

```python
import jax
import jax.numpy as jnp
from jax import lax
from jax.experimental import pallas as pl
from jax.experimental.pallas import tpu as pltpu
from jax.sharding import Mesh
from jax.sharding import PartitionSpec as P

TILE = 128
SIZES = {"y": 4, "z": 8, "x": 4, "core": 2}
ROW = ("y", "z")
COL = ("x", "core")
VM = pltpu.VMEM
F32 = jnp.float32
BF16 = jnp.bfloat16
STEPS = (0, 1, 2, -1)


def from_ahead(value, axis, k):
    n = SIZES[axis]
    return lax.ppermute(value, axis, [((i + k) % n, i) for i in range(n)])


def to_ahead(value, axis, k):
    n = SIZES[axis]
    return lax.ppermute(value, axis, [(i, (i + k) % n) for i in range(n)])


def call(body, outs, smem, vmem, flops=0, scratch=(), limit=24):
    outs = [jax.ShapeDtypeStruct(s, d) for s, d in outs]
    return pl.pallas_call(
        body,
        out_shape=outs,
        in_specs=[pl.BlockSpec(memory_space=pltpu.SMEM)] * len(smem)
        + [pl.BlockSpec(memory_space=VM)] * len(vmem),
        out_specs=[pl.BlockSpec(memory_space=VM)] * len(outs),
        scratch_shapes=list(scratch),
        compiler_params=pltpu.CompilerParams(vmem_limit_bytes=limit * 2**20),
        cost_estimate=pl.CostEstimate(
            flops=flops,
            transcendentals=0,
            bytes_accessed=sum(v.size * v.dtype.itemsize for v in vmem)
            + sum(o.size * o.dtype.itemsize for o in outs),
        ),
    )(*smem, *vmem)


def tile_ref(ref, r, c):
    return ref.at[
        pl.ds(pl.multiple_of(r * TILE, TILE), TILE), pl.ds(pl.multiple_of(c * TILE, TILE), TILE)
    ]


def mask_body(rows, cols, count, w, out, flipped):
    out[...] = jnp.zeros_like(out)
    flipped[...] = jnp.zeros_like(flipped)

    @pl.loop(0, count[0])
    def _(k):
        tile = tile_ref(w, rows[k], cols[k])[...]
        tile_ref(out, rows[k], cols[k])[...] = tile
        tile_ref(flipped, cols[k], rows[k])[...] = tile.T


def zpos(pos, i, hi):
    return (pos[1] + i + 4 * hi + 8) % 8


def up_part(pos, toks, w, at, keep, send, acc):
    core = pos[3]

    @pl.loop(0, 4)
    def _(d):
        part = jnp.dot(
            toks[d].reshape(-1, toks.shape[-1]), w[:, at], preferred_element_type=F32
        )
        acc[...] = part.reshape(acc.shape)
        keep[d] = acc[core]
        send[d] = acc[1 - core].astype(BF16)


def up_first_body(pos, *refs):
    a3, b3, w = refs[:4], refs[4:8], refs[8]
    keep, send, toks, acc = refs[9:]
    cut = a3[0].shape[-1]
    back = pos[0] - pos[2] + 4
    for j in range(4):
        d = (j + back) % 4
        for i in range(4):
            for hi in range(2):
                at = zpos(pos, STEPS[i], hi)
                toks[d, at, :, :cut] = a3[i][j, hi]
                toks[d, at, :, cut:] = b3[j][i, hi]
    up_part(pos, toks, w, slice(0, keep.shape[-1]), keep, send, acc)


def up_second_body(pos, toks, w, keep, send, acc):
    n = keep.shape[-1]
    up_part(pos, toks, w, slice(n, 2 * n), keep, send, acc)


def collect(pos, mine, other, slots, sems):
    core = pos[3]
    copies = [
        pltpu.make_async_copy(g, slots(side), sems.at[s])
        for s, (side, g) in enumerate(((core, mine), (1 - core, other)))
    ]
    for c in copies:
        c.start()
    for c in copies:
        c.wait()


def back_first_body(pos, *refs):
    mine, other, w, total, grads, sems = refs
    collect(pos, mine, other, lambda side: grads.at[:, side], sems)

    @pl.loop(0, 4)
    def _(d):
        g = grads[d].reshape(-1, grads.shape[-1])
        part = jnp.dot(g, w[: g.shape[1]], preferred_element_type=F32)
        total[d] = part.reshape(total.shape[1:])


def back_second_body(pos, *refs):
    mine, other, w, total, first = refs[:5]
    a3, b3, grads = refs[5:9], refs[9:13], refs[13]
    acc, sems, first_sem = refs[14:]
    cut = first.shape[-1]
    kept = pltpu.make_async_copy(first, grads.at[:, :, :, pl.ds(0, cut)], first_sem)
    kept.start()
    collect(pos, mine, other, lambda side: grads.at[:, side, :, pl.ds(cut, cut)], sems)
    back = pos[0] - pos[2] + 4

    @pl.loop(0, 4)
    def _(j):
        d = (j + back) % 4
        g = grads[d, :, :, cut:].reshape(-1, cut)
        part = jnp.dot(g, w[cut:], preferred_element_type=F32)
        acc[j] = total[d] + part.reshape(total.shape[1:])

    kept.wait()
    cut = a3[0].shape[-1]
    for hi in range(2):
        for k in range(4):

            @pl.loop(0, 4)
            def _(j, k=k, hi=hi):
                piece = acc[j, zpos(pos, STEPS[k], hi), :, :cut]
                a3[k][j, hi] = piece.astype(a3[k].dtype)

            @pl.loop(0, 4)
            def _(i, k=k, hi=hi):
                piece = acc[k, zpos(pos, jnp.where(i == 3, -1, i), hi), :, cut:]
                b3[k][i, hi] = piece.astype(b3[k].dtype)


def add_body(keep, recv, *out):
    for d in range(4):

        @pl.loop(0, keep.shape[1] // 32)
        def _(i, d=d):
            at = pl.ds(pl.multiple_of(i * 32, 32), 32)
            total = keep[d, at] + recv[d, at].astype(F32)
            out[d][at] = total.astype(out[d].dtype)


def act_body(own, r1, r2, r3, cot, hidden, grad_pre):
    @pl.loop(0, own.shape[0] // 32)
    def _(i):
        at = pl.ds(pl.multiple_of(i * 32, 32), 32)
        pre_act = own[at] + r1[at].astype(F32) + r2[at].astype(F32) + r3[at].astype(F32)
        gate = jax.nn.sigmoid(pre_act)
        hidden[at] = (pre_act * gate).astype(BF16)
        slope = gate * (1.0 + pre_act * (1.0 - gate))
        grad_pre[at] = (cot[at].astype(F32) * slope).astype(BF16)


def wgrad_body(rows, cols, count, toks, grads, out, acc):
    acc[...] = jnp.zeros_like(acc)
    step = 256

    @pl.loop(0, 4)
    def _(d):
        t = toks[d].reshape(-1, toks.shape[-1])

        @pl.loop(0, acc.shape[1] // step)
        def _(k):
            at = pl.ds(pl.multiple_of(k * step, step), step)
            g = grads[d, :, :, at].reshape(-1, step)
            acc[:, at] += lax.dot_general(
                t, g, (((0,), (0,)), ((), ())), preferred_element_type=F32
            )

    out[...] = jnp.zeros_like(out)

    @pl.loop(0, count[0])
    def _(k):
        tile_ref(out, rows[k], cols[k])[...] = tile_ref(acc, rows[k], cols[k])[...].astype(BF16)


def gather_four(piece, axis):
    return [piece] + [from_ahead(piece, axis, k) for k in STEPS[1:]]


def gather_tokens(tokens):
    pair = jnp.stack([tokens, from_ahead(tokens, "z", 4)])
    cut = tokens.shape[1] // 2
    a2 = gather_four(pair[:, :, :cut], "y")
    b2 = gather_four(pair[:, :, cut:], "z")
    a2, b2 = lax.optimization_barrier((a2, b2))
    return gather_four(jnp.stack(a2), "z"), gather_four(jnp.stack(b2), "y")


def partial_sums(keep, send):
    shape = keep.shape[1:]
    return call(
        add_body, [(shape, F32)] + [(shape, BF16)] * 3, [], [keep, to_ahead(send, "core", 1)]
    )


def shares(sends):
    return [to_ahead(s, "x", d + 1) for d, s in enumerate(sends)]


def activation(own, recvs, cot):
    return call(act_body, [(own.shape, BF16)] * 2, [], [own] + recvs + [cot])


def gather_grads(grad_pre):
    mine = jnp.stack([grad_pre] + [from_ahead(grad_pre, "x", d) for d in range(1, 4)])
    return [mine, to_ahead(mine, "core", 1)]


def reduce_four(own, sends, axis):
    total = own
    for k, s in zip(STEPS[1:], sends):
        total = total + to_ahead(s.astype(BF16), axis, k).astype(F32)
    return total


def middle(a3, b3, wm, flipped, pos, cot):
    rows = a3[0].shape[2] * 4
    depth, width = wm.shape
    cut = width // 2
    flops = 8 * rows * depth * width
    pair = [((4, rows, cut), F32), ((4, rows, cut), BF16)]
    tok_shape = ((4, 8, rows // 4, depth), BF16)
    acc = VM((2, rows, cut), F32)
    keep1, send1, toks = call(
        up_first_body, pair + [tok_shape], [pos], a3 + b3 + [wm], flops, [acc]
    )
    own1, *sends1 = partial_sums(keep1, send1)
    keep2, send2 = call(up_second_body, pair, [pos], [toks, wm], flops, [acc])
    own2, *sends2 = partial_sums(keep2, send2)
    hidden1, grad1 = activation(own1, shares(sends1), cot[:, :cut])
    hidden2, grad2 = activation(own2, shares(sends2), cot[:, cut:])
    parts1 = gather_grads(grad1)
    parts2 = gather_grads(grad2)
    g_shape = ((4, 2, rows, cut), BF16)
    sems = pltpu.SemaphoreType.DMA((2,))
    sums = (4, 8, rows // 4, depth)
    total, g1 = call(
        back_first_body, [(sums, F32), g_shape], [pos], parts1 + [flipped], flops, [sems]
    )
    shape = (4, 2, rows // 4, depth // 2)
    outs = [(shape, F32)] + [(shape, BF16)] * 3
    *sends, grads = call(
        back_second_body,
        outs + outs + [((4, 2, rows, width), BF16)],
        [pos],
        parts2 + [flipped, total, g1],
        flops,
        [VM(sums, F32), sems, pltpu.SemaphoreType.DMA],
    )
    hidden = jnp.concatenate([hidden1, hidden2], axis=1)
    return hidden, sends, toks, grads


def reduce_inputs(sends, weight_grad):
    a2 = reduce_four(sends[0], sends[1:4], "z")
    b2 = reduce_four(sends[4], sends[5:], "y")
    a2, b2, weight_grad = lax.optimization_barrier((a2, b2, weight_grad))
    a1 = reduce_four(a2[0], a2[1:], "y")
    b1 = reduce_four(b2[0], b2[1:], "z")
    both = jnp.concatenate([a1, b1], axis=-1)
    total = both[0] + to_ahead(both[1].astype(BF16), "z", 4).astype(F32)
    return total.astype(BF16), weight_grad


def on_device(tokens, weight, tile_rows, tile_cols, tile_count, hidden_cotangent):
    y, z, x, core = (lax.axis_index(a) for a in ("y", "z", "x", "core"))
    pos = jnp.stack([y, z, x, core]).astype(jnp.int32)
    row_blocks = weight.shape[0] // TILE
    col_blocks = weight.shape[1] // TILE
    rows = tile_rows.reshape(-1) - (x * 2 + core) * row_blocks
    cols = tile_cols.reshape(-1) - (y * 8 + z) * col_blocks
    count = tile_count.reshape(1)
    shapes = [(weight.shape, BF16), (weight.shape[::-1], BF16)]
    wm, flipped = call(mask_body, shapes, [rows, cols, count], [weight])
    a3, b3 = gather_tokens(tokens)
    hidden, sends, toks, grads = middle(a3, b3, wm, flipped, pos, hidden_cotangent)
    (weight_grad,) = call(
        wgrad_body,
        [(weight.shape, BF16)],
        [rows, cols, count],
        [toks, grads],
        2 * 1536 * weight.size,
        [VM(weight.shape, F32)],
    )
    input_grad, weight_grad = reduce_inputs(sends, weight_grad)
    return hidden, input_grad, weight_grad


def solution(mesh):
    split = Mesh(mesh.devices.reshape(4, 8, 4, 2), ("y", "z", "x", "core"))
    return jax.shard_map(
        on_device,
        mesh=split,
        in_specs=(
            P(ROW, COL),
            P(COL, ROW),
            P(ROW, COL, None),
            P(ROW, COL, None),
            P(ROW, COL),
            P(COL, ROW),
        ),
        out_specs=(P(COL, ROW), P(ROW, COL), P(COL, ROW)),
        check_vma=False,
    )
```

```python
import functools

import jax
import jax.numpy as jnp
from jax import lax
from jax.experimental import pallas as pl
from jax.experimental.pallas import tpu as pltpu
from jax.sharding import Mesh
from jax.sharding import PartitionSpec as P

TILE = 128
SIZES = {"y": 4, "z": 8, "x": 4, "core": 2}
ROW = ("y", "z")
COL = ("x", "core")
VM = pltpu.VMEM
F32 = jnp.float32
BF16 = jnp.bfloat16
STEPS = (0, 1, 2, -1)


def from_ahead(value, axis, k):
    n = SIZES[axis]
    return lax.ppermute(value, axis, [((i + k) % n, i) for i in range(n)])


def to_ahead(value, axis, k):
    n = SIZES[axis]
    return lax.ppermute(value, axis, [(i, (i + k) % n) for i in range(n)])


def call(body, outs, smem, vmem, flops=0, scratch=(), limit=24):
    outs = [jax.ShapeDtypeStruct(s, d) for s, d in outs]
    return pl.pallas_call(
        body,
        out_shape=outs,
        in_specs=[pl.BlockSpec(memory_space=pltpu.SMEM)] * len(smem)
        + [pl.BlockSpec(memory_space=VM)] * len(vmem),
        out_specs=[pl.BlockSpec(memory_space=VM)] * len(outs),
        scratch_shapes=list(scratch),
        compiler_params=pltpu.CompilerParams(vmem_limit_bytes=limit * 2**20),
        cost_estimate=pl.CostEstimate(
            flops=flops,
            transcendentals=0,
            bytes_accessed=sum(v.size * v.dtype.itemsize for v in vmem)
            + sum(o.size * o.dtype.itemsize for o in outs),
        ),
    )(*smem, *vmem)


def tile_ref(ref, r, c):
    return ref.at[
        pl.ds(pl.multiple_of(r * TILE, TILE), TILE), pl.ds(pl.multiple_of(c * TILE, TILE), TILE)
    ]


def mask_body(rows, cols, count, w, out, flipped):
    out[...] = jnp.zeros_like(out)
    flipped[...] = jnp.zeros_like(flipped)

    @pl.loop(0, count[0])
    def _(k):
        tile = tile_ref(w, rows[k], cols[k])[...]
        tile_ref(out, rows[k], cols[k])[...] = tile
        tile_ref(flipped, cols[k], rows[k])[...] = tile.T


def zpos(pos, i, hi):
    return (pos[1] + i + 4 * hi + 8) % 8


def z_step(i, j):
    return -2 if i == 2 and j >= 2 else STEPS[i]


def at_step(pieces, step, k):
    if step == 2:
        return pieces[2 + k // 2], k % 2
    return pieces[step + step // 3], k


def up_body(pos, *refs):
    a3, b3, w = refs[:5], refs[5:10], refs[10]
    keep, send, toks, acc = refs[11:]
    core = pos[3]
    cut = a3[0].shape[-1]
    back = pos[0] - pos[2] + 4
    for j in range(4):
        d = (j + back) % 4
        for i in range(4):
            a_ref, a_at = at_step(a3, i, j)
            b_ref, b_at = at_step(b3, j, i)
            for hi in range(2):
                at = zpos(pos, STEPS[i], hi)
                low = zpos(pos, z_step(i, j), hi)
                toks[d, low, :, :cut] = a_ref[a_at, hi]
                toks[d, at, :, cut:] = b_ref[b_at, hi]

    @pl.loop(0, 4)
    def _(d):
        part = jnp.dot(
            toks[d].reshape(-1, toks.shape[-1]), w[...], preferred_element_type=F32
        )
        acc[...] = part.reshape(acc.shape)
        keep[d] = acc[core]
        send[d] = acc[1 - core].astype(BF16)


def collect(pos, mine, other, slots, sems):
    core = pos[3]
    copies = [
        pltpu.make_async_copy(g, slots(side), sems.at[s])
        for s, (side, g) in enumerate(((core, mine), (1 - core, other)))
    ]
    for c in copies:
        c.start()
    for c in copies:
        c.wait()


def back_first_body(pos, *refs):
    mine, other, w, total, grads, sems = refs
    collect(pos, mine, other, lambda side: grads.at[:, side], sems)

    @pl.loop(0, 4)
    def _(d):
        g = grads[d].reshape(-1, grads.shape[-1])
        part = jnp.dot(g, w[: g.shape[1]], preferred_element_type=F32)
        total[d] = part.reshape(total.shape[1:])


def back_second_body(pos, *refs):
    mine, other, w, total, first = refs[:5]
    a3, b3, grads = refs[5:9], refs[9:13], refs[13]
    acc, sems, first_sem = refs[14:]
    cut = first.shape[-1]
    kept = pltpu.make_async_copy(first, grads.at[:, :, :, pl.ds(0, cut)], first_sem)
    kept.start()
    collect(pos, mine, other, lambda side: grads.at[:, side, :, pl.ds(cut, cut)], sems)
    back = pos[0] - pos[2] + 4

    @pl.loop(0, 4)
    def _(j):
        d = (j + back) % 4
        g = grads[d, :, :, cut:].reshape(-1, cut)
        part = jnp.dot(g, w[cut:], preferred_element_type=F32)
        acc[j] = total[d] + part.reshape(total.shape[1:])

    kept.wait()
    cut = a3[0].shape[-1]
    for hi in range(2):
        for k in range(4):

            @pl.loop(0, 4)
            def _(j, k=k, hi=hi):
                step = jnp.where(j >= 2, z_step(k, 2), z_step(k, 0))
                piece = acc[j, zpos(pos, step, hi), :, :cut]
                a3[k][j, hi] = piece.astype(a3[k].dtype)

            @pl.loop(0, 4)
            def _(i, k=k, hi=hi):
                piece = acc[k, zpos(pos, jnp.where(i == 3, -1, i), hi), :, cut:]
                b3[k][i, hi] = piece.astype(b3[k].dtype)


def add_body(cols, keep, recv, *out):
    for d in range(4):

        @pl.loop(0, keep.shape[1] // 32)
        def _(i, d=d):
            at = pl.ds(pl.multiple_of(i * 32, 32), 32)
            total = keep[d, at, cols] + recv[d, at, cols].astype(F32)
            out[d][at] = total.astype(out[d].dtype)


def act_body(own, r1, r2, r3, cot, hidden, grad_pre):
    @pl.loop(0, own.shape[0] // 32)
    def _(i):
        at = pl.ds(pl.multiple_of(i * 32, 32), 32)
        pre_act = own[at] + r1[at].astype(F32) + r2[at].astype(F32) + r3[at].astype(F32)
        gate = jax.nn.sigmoid(pre_act)
        hidden[at] = (pre_act * gate).astype(BF16)
        slope = gate * (1.0 + pre_act * (1.0 - gate))
        grad_pre[at] = (cot[at].astype(F32) * slope).astype(BF16)


def wgrad_body(rows, cols, count, toks, grads, out, acc):
    acc[...] = jnp.zeros_like(acc)
    step = 512

    @pl.loop(0, 4)
    def _(d):
        t = toks[d].reshape(-1, toks.shape[-1])

        @pl.loop(0, acc.shape[1] // step)
        def _(k):
            at = pl.ds(pl.multiple_of(k * step, step), step)
            g = grads[d, :, :, at].reshape(-1, step)
            acc[:, at] += lax.dot_general(
                t, g, (((0,), (0,)), ((), ())), preferred_element_type=F32
            )

    out[...] = jnp.zeros_like(out)

    @pl.loop(0, count[0])
    def _(k):
        tile_ref(out, rows[k], cols[k])[...] = tile_ref(acc, rows[k], cols[k])[...].astype(BF16)


def gather_four(piece, axis):
    return [piece] + [from_ahead(piece, axis, k) for k in STEPS[1:]]


def ring_gather(piece, axis):
    ahead, behind = from_ahead(piece, axis, 1), from_ahead(piece, axis, -1)
    half = piece.shape[0] // 2
    far = [from_ahead(ahead[:half], axis, 1), from_ahead(behind[half:], axis, -1)]
    return [piece, ahead] + far + [behind]


def gather_tokens(tokens):
    pair = jnp.stack([tokens, from_ahead(tokens, "z", 4)])
    cut = tokens.shape[1] // 2
    a2 = gather_four(pair[:, :, :cut], "y")
    b2 = gather_four(pair[:, :, cut:], "z")
    a2, b2 = lax.optimization_barrier((a2, b2))
    return ring_gather(jnp.stack(a2), "z"), ring_gather(jnp.stack(b2), "y")


def partial_sums(keep, recv, cols):
    shape = (keep.shape[1], cols.stop - cols.start)
    body = functools.partial(add_body, cols)
    return call(body, [(shape, F32)] + [(shape, BF16)] * 3, [], [keep, recv])


def shares(sends):
    return [to_ahead(s, "x", d + 1) for d, s in enumerate(sends)]


def activation(own, recvs, cot):
    return call(act_body, [(own.shape, BF16)] * 2, [], [own] + recvs + [cot])


def gather_grads(grad_pre):
    mine = jnp.stack([grad_pre] + [from_ahead(grad_pre, "x", d) for d in range(1, 4)])
    return [mine, to_ahead(mine, "core", 1)]


def reduce_four(own, sends, axis):
    total = own
    for k, s in zip(STEPS[1:], sends):
        total = total + to_ahead(s.astype(BF16), axis, k).astype(F32)
    return total


def ring_reduce(own, ahead, far, behind, axis):
    half = own.shape[0] // 2
    lo = to_ahead(far[:half], axis, 1).astype(F32)
    hi = to_ahead(far[half:], axis, -1).astype(F32)
    ahead = jnp.concatenate([ahead[:half] + lo, ahead[half:]])
    behind = jnp.concatenate([behind[:half], behind[half:] + hi])
    total = own + to_ahead(ahead.astype(BF16), axis, 1).astype(F32)
    return total + to_ahead(behind.astype(BF16), axis, -1).astype(F32)


def middle(a3, b3, wm, flipped, pos, cot):
    rows = a3[0].shape[2] * 4
    depth, width = wm.shape
    cut = width // 2
    flops = 8 * rows * depth * width
    keep, send, toks = call(
        up_body,
        [
            ((4, rows, width), F32),
            ((4, rows, width), BF16),
            ((4, 8, rows // 4, depth), BF16),
        ],
        [pos],
        a3 + b3 + [wm],
        2 * flops,
        [VM((2, rows, width), F32)],
    )
    recv = to_ahead(send, "core", 1)
    own1, *sends1 = partial_sums(keep, recv, slice(0, cut))
    own2, *sends2 = partial_sums(keep, recv, slice(cut, width))
    hidden1, grad1 = activation(own1, shares(sends1), cot[:, :cut])
    hidden2, grad2 = activation(own2, shares(sends2), cot[:, cut:])
    parts1 = gather_grads(grad1)
    parts2 = gather_grads(grad2)
    g_shape = ((4, 2, rows, cut), BF16)
    sems = pltpu.SemaphoreType.DMA((2,))
    sums = (4, 8, rows // 4, depth)
    total, g1 = call(
        back_first_body, [(sums, F32), g_shape], [pos], parts1 + [flipped], flops, [sems]
    )
    shape = (4, 2, rows // 4, depth // 2)
    outs = [(shape, d) for d in (F32, F32, BF16, F32)]
    *sends, grads = call(
        back_second_body,
        outs + outs + [((4, 2, rows, width), BF16)],
        [pos],
        parts2 + [flipped, total, g1],
        flops,
        [VM(sums, F32), sems, pltpu.SemaphoreType.DMA],
    )
    hidden = jnp.concatenate([hidden1, hidden2], axis=1)
    return hidden, sends, toks, grads


def reduce_inputs(sends):
    a2 = ring_reduce(*sends[:4], "z")
    b2 = ring_reduce(*sends[4:], "y")
    a2, b2 = lax.optimization_barrier((a2, b2))
    a1 = reduce_four(a2[0], a2[1:], "y")
    b1 = reduce_four(b2[0], b2[1:], "z")
    both = jnp.concatenate([a1, b1], axis=-1)
    total = both[0] + to_ahead(both[1].astype(BF16), "z", 4).astype(F32)
    return total.astype(BF16)


def on_device(tokens, weight, tile_rows, tile_cols, tile_count, hidden_cotangent):
    y, z, x, core = (lax.axis_index(a) for a in ("y", "z", "x", "core"))
    pos = jnp.stack([y, z, x, core]).astype(jnp.int32)
    row_blocks = weight.shape[0] // TILE
    col_blocks = weight.shape[1] // TILE
    rows = tile_rows.reshape(-1) - (x * 2 + core) * row_blocks
    cols = tile_cols.reshape(-1) - (y * 8 + z) * col_blocks
    count = tile_count.reshape(1)
    shapes = [(weight.shape, BF16), (weight.shape[::-1], BF16)]
    wm, flipped = call(mask_body, shapes, [rows, cols, count], [weight])
    a3, b3 = gather_tokens(tokens)
    hidden, sends, toks, grads = middle(a3, b3, wm, flipped, pos, hidden_cotangent)
    (weight_grad,) = call(
        wgrad_body,
        [(weight.shape, BF16)],
        [rows, cols, count],
        [toks, grads],
        2 * 1536 * weight.size,
        [VM(weight.shape, F32)],
    )
    input_grad = reduce_inputs(sends)
    return hidden, input_grad, weight_grad


def solution(mesh):
    split = Mesh(mesh.devices.reshape(4, 8, 4, 2), ("y", "z", "x", "core"))
    return jax.shard_map(
        on_device,
        mesh=split,
        in_specs=(
            P(ROW, COL),
            P(COL, ROW),
            P(ROW, COL, None),
            P(ROW, COL, None),
            P(ROW, COL),
            P(COL, ROW),
        ),
        out_specs=(P(COL, ROW), P(ROW, COL), P(COL, ROW)),
        check_vma=False,
    )
```

```python
import functools

import jax
import jax.numpy as jnp
from jax import lax
from jax.experimental import pallas as pl
from jax.experimental.pallas import tpu as pltpu
from jax.sharding import Mesh
from jax.sharding import PartitionSpec as P

TILE = 128
SIZES = {"y": 4, "z": 8, "x": 4, "core": 2}
ROW = ("y", "z")
COL = ("x", "core")
VM = pltpu.VMEM
F32 = jnp.float32
BF16 = jnp.bfloat16
STEPS = (0, 1, 2, -1)


def from_ahead(value, axis, k):
    n = SIZES[axis]
    return lax.ppermute(value, axis, [((i + k) % n, i) for i in range(n)])


def to_ahead(value, axis, k):
    n = SIZES[axis]
    return lax.ppermute(value, axis, [(i, (i + k) % n) for i in range(n)])


def call(body, outs, smem, vmem, flops=0, scratch=(), limit=24):
    outs = [jax.ShapeDtypeStruct(s, d) for s, d in outs]
    return pl.pallas_call(
        body,
        out_shape=outs,
        in_specs=[pl.BlockSpec(memory_space=pltpu.SMEM)] * len(smem)
        + [pl.BlockSpec(memory_space=VM)] * len(vmem),
        out_specs=[pl.BlockSpec(memory_space=VM)] * len(outs),
        scratch_shapes=list(scratch),
        compiler_params=pltpu.CompilerParams(vmem_limit_bytes=limit * 2**20),
        cost_estimate=pl.CostEstimate(
            flops=flops,
            transcendentals=0,
            bytes_accessed=sum(v.size * v.dtype.itemsize for v in vmem)
            + sum(o.size * o.dtype.itemsize for o in outs),
        ),
    )(*smem, *vmem)


def tile_ref(ref, r, c):
    return ref.at[
        pl.ds(pl.multiple_of(r * TILE, TILE), TILE), pl.ds(pl.multiple_of(c * TILE, TILE), TILE)
    ]


def mask_body(rows, cols, count, w, out, flipped):
    out[...] = jnp.zeros_like(out)
    flipped[...] = jnp.zeros_like(flipped)

    @pl.loop(0, count[0])
    def _(k):
        tile = tile_ref(w, rows[k], cols[k])[...]
        tile_ref(out, rows[k], cols[k])[...] = tile
        tile_ref(flipped, cols[k], rows[k])[...] = tile.T


def z_half(pos, step):
    return ((pos[1] + step + 8) % 8) // 4


def turned(pos):
    return pos[0] - pos[2] + 4


def up_body(steps, pos, *refs):
    pieces, w = refs[:5], refs[5]
    keep, send, toks = refs[6:]
    core = pos[3]
    for j in range(4):
        d = (j + turned(pos)) % 4
        for i, step in enumerate(steps):
            ref, at = (pieces[2 + i], 0) if j == 2 else (pieces[j + j // 3], i)
            for hi in range(2):
                side = (z_half(pos, step) + hi + core) % 2
                toks[d, side, i] = ref[at, hi]

    @pl.loop(0, 2)
    def _(k):
        at = pl.ds(k * 2, 2)
        part = jnp.dot(
            toks[at].reshape(-1, toks.shape[-1]), w[...], preferred_element_type=F32
        )
        part = part.reshape(2, 2, keep.shape[1], keep.shape[2])
        keep[at] = part[:, 0]
        send[at] = part[:, 1].astype(BF16)


def add_body(keep, recv, *out):
    for d in range(4):

        @pl.loop(0, keep.shape[1] // 16)
        def _(i, d=d):
            at = pl.ds(pl.multiple_of(i * 16, 16), 16)
            total = keep[d, at] + recv[d, at].astype(F32)
            out[d][at] = total.astype(out[d].dtype)


def act_body(steps, pos, own, r1, r2, r3, cot, *refs):
    hidden, grad_pre = refs[-2:]
    whole = len(refs) == 3
    size = cot.shape[1]
    for i, step in enumerate(steps):
        block = (pos[1] + step + 8) % 4

        @pl.loop(0, size // 16)
        def _(k, i=i, block=block):
            here = pl.ds(pl.multiple_of(k * 16, 16), 16)
            at = pl.ds(pl.multiple_of(i * size + k * 16, 16), 16)
            pre_act = own[at] + r1[at].astype(F32) + r2[at].astype(F32) + r3[at].astype(F32)
            gate = jax.nn.sigmoid(pre_act)
            hidden[block if whole else i, here] = (pre_act * gate).astype(BF16)
            slope = gate * (1.0 + pre_act * (1.0 - gate))
            grad_pre[at] = (cot[block, here].astype(F32) * slope).astype(BF16)

    if whole:
        for i, step in enumerate(STEPS[:2]):
            hidden[(pos[1] + step + 8) % 4] = refs[0][i]


def back_body(steps, pos, mine, other, w, own, ahead, far, behind, grads, acc, sems):
    core = pos[3]
    copies = [
        pltpu.make_async_copy(g, grads.at[:, side], sems.at[side])
        for side, g in enumerate((mine, other))
    ]
    for c in copies:
        c.start()
    for c in copies:
        c.wait()

    @pl.loop(0, 2)
    def _(k):
        at = pl.ds(k * 2, 2)
        part = jnp.dot(
            grads[at].reshape(-1, grads.shape[-1]), w[...], preferred_element_type=F32
        )
        acc[at] = part.reshape(2, 2, 2, acc.shape[3], acc.shape[4])

    for j, out in enumerate((own, ahead, far, behind)):
        d = (j + turned(pos)) % 4
        for i, step in enumerate(steps):

            @pl.loop(0, 2)
            def _(side, i=i, step=step, d=d, out=out):
                part = acc[d, side, i]
                out[i, (z_half(pos, step) + side + core) % 2] = part.astype(out.dtype)


def wgrad_body(rows, cols, count, t1, g1, t2, g2, out, acc):
    acc[...] = jnp.zeros_like(acc)
    for toks, grads in ((t1, g1), (t2, g2)):

        @pl.loop(0, 2)
        def _(k, toks=toks, grads=grads):
            at = pl.ds(k * 2, 2)
            t = toks[at].reshape(-1, toks.shape[-1])
            g = grads[at].reshape(-1, grads.shape[-1])
            acc[...] += lax.dot_general(
                t, g, (((0,), (0,)), ((), ())), preferred_element_type=F32
            )

    out[...] = jnp.zeros_like(out)

    @pl.loop(0, count[0])
    def _(k):
        tile_ref(out, rows[k], cols[k])[...] = tile_ref(acc, rows[k], cols[k])[...].astype(BF16)


def both_sides(piece, axis):
    return [from_ahead(piece, axis, 1), from_ahead(piece, axis, -1)]


def far_halves(ahead, behind, axis):
    half = ahead.shape[0] // 2
    return [from_ahead(ahead[:half], axis, 1), from_ahead(behind[half:], axis, -1)]


def after(values, *others):
    return lax.optimization_barrier((values, others))[0]


def far_shares(far, axis):
    half = far.shape[0] // 2
    return [to_ahead(far[:half], axis, 1), to_ahead(far[half:], axis, -1)]


def ring_reduce(own, ahead, behind, shares, axis):
    half = own.shape[0] // 2
    lo, hi = (s.astype(F32) for s in shares)
    ahead = jnp.concatenate([ahead[:half] + lo, ahead[half:]])
    behind = jnp.concatenate([behind[:half], behind[half:] + hi])
    total = own + to_ahead(ahead.astype(BF16), axis, 1).astype(F32)
    return total + to_ahead(behind.astype(BF16), axis, -1).astype(F32)


def up(pieces, steps, wm, pos):
    rows = 2 * pieces[0].shape[2]
    depth, width = wm.shape
    keep, send, toks = call(
        functools.partial(up_body, steps),
        [
            ((4, rows, width), F32),
            ((4, rows, width), BF16),
            ((4, 2, 2, rows // 2, depth), BF16),
        ],
        [pos],
        pieces + [wm],
        16 * rows * depth * width,
    )
    shape = (rows, width)
    recv = to_ahead(send, "core", 1)
    own, *sends = call(add_body, [(shape, F32)] + [(shape, BF16)] * 3, [], [keep, recv])
    return own, sends, toks


def activation(own, sends, cot, steps, pos, before):
    recvs = [to_ahead(s, "x", d + 1) for d, s in enumerate(sends)]
    out = (4 if before else 2,) + cot.shape[1:]
    return call(
        functools.partial(act_body, steps),
        [(out, BF16), (own.shape, BF16)],
        [pos],
        [own] + recvs + [cot] + before,
    )


def gather_grads(grad_pre):
    mine = jnp.stack([grad_pre] + [from_ahead(grad_pre, "x", d) for d in range(1, 4)])
    return mine, to_ahead(mine, "core", 1)


def back(mine, other, steps, flipped, pos):
    rows, width = mine.shape[1:]
    depth = flipped.shape[1]
    shape = (2, 2, rows // 2, depth)
    *sends, grads = call(
        functools.partial(back_body, steps),
        [(shape, d) for d in (F32, F32, BF16, F32)] + [((4, 2, rows, width), BF16)],
        [pos],
        [mine, other, flipped],
        16 * rows * depth * width,
        [VM((4,) + shape, F32), pltpu.SemaphoreType.DMA((2,))],
    )
    return sends, grads


def on_device(tokens, weight, tile_rows, tile_cols, tile_count, hidden_cotangent):
    y, z, x, core = (lax.axis_index(a) for a in ("y", "z", "x", "core"))
    pos = jnp.stack([y, z, x, core]).astype(jnp.int32)
    row_blocks = weight.shape[0] // TILE
    col_blocks = weight.shape[1] // TILE
    rows = tile_rows.reshape(-1) - (x * 2 + core) * row_blocks
    cols = tile_cols.reshape(-1) - (y * 8 + z) * col_blocks
    count = tile_count.reshape(1)
    shapes = [(weight.shape, BF16), (weight.shape[::-1], BF16)]
    wm, flipped = call(mask_body, shapes, [rows, cols, count], [weight])
    pair = jnp.stack([tokens, from_ahead(tokens, "z", 4)])
    pairs = [pair] + [from_ahead(pair, "z", k) for k in STEPS[1:]]
    cot = hidden_cotangent.reshape(4, tokens.shape[0], -1)
    first, second = STEPS[:2], STEPS[2:]
    piece1, piece2 = jnp.stack(pairs[:2]), jnp.stack(pairs[2:])
    ahead1, behind1 = both_sides(piece1, "y")
    far1 = far_halves(*after((ahead1, behind1), piece2), "y")
    ahead2, behind2 = both_sides(after(piece2, ahead1, behind1), "y")
    own1, sends1, toks1 = up([piece1, ahead1] + far1 + [behind1], first, wm, pos)
    ahead2, behind2 = after((ahead2, behind2), toks1)
    far2 = far_halves(ahead2, behind2, "y")
    own2, sends2, toks2 = up([piece2, ahead2] + far2 + [behind2], second, wm, pos)
    hidden1, grad1 = activation(own1, sends1, cot, first, pos, [])
    sends2 = after(sends2, grad1)
    parts1, grads1 = back(*gather_grads(grad1), first, flipped, pos)
    shares1 = far_shares(parts1[2], "y")
    own2 = after(own2, shares1)
    hidden, grad2 = activation(own2, sends2, cot, second, pos, [hidden1])
    sums1 = ring_reduce(parts1[0], parts1[1], parts1[3], shares1, "y")
    mine2, other2 = after(gather_grads(grad2), sums1)
    parts2, grads2 = back(mine2, other2, second, flipped, pos)
    sums2 = ring_reduce(parts2[0], parts2[1], parts2[3], far_shares(parts2[2], "y"), "y")
    total = sums1[0]
    for k, piece in zip(STEPS[1:], (sums1[1], sums2[0], sums2[1])):
        total = total + to_ahead(piece.astype(BF16), "z", k).astype(F32)
    input_grad = total[0] + to_ahead(total[1].astype(BF16), "z", 4).astype(F32)
    (weight_grad,) = call(
        wgrad_body,
        [(weight.shape, BF16)],
        [rows, cols, count],
        [
            toks1.reshape(4, -1, weight.shape[0]),
            grads1.reshape(4, -1, weight.shape[1]),
            toks2.reshape(4, -1, weight.shape[0]),
            grads2.reshape(4, -1, weight.shape[1]),
        ],
        2 * 1536 * weight.size,
        [VM(weight.shape, F32)],
    )
    return hidden.reshape(hidden_cotangent.shape), input_grad.astype(BF16), weight_grad


def solution(mesh):
    split = Mesh(mesh.devices.reshape(4, 8, 4, 2), ("y", "z", "x", "core"))
    return jax.shard_map(
        on_device,
        mesh=split,
        in_specs=(
            P(ROW, COL),
            P(COL, ROW),
            P(ROW, COL, None),
            P(ROW, COL, None),
            P(ROW, COL),
            P(COL, ROW),
        ),
        out_specs=(P(COL, ROW), P(ROW, COL), P(COL, ROW)),
        check_vma=False,
    )
```

```python
import jax
import jax.numpy as jnp
from jax import lax
from jax.experimental import pallas as pl
from jax.experimental.pallas import tpu as pltpu
from jax.sharding import Mesh
from jax.sharding import PartitionSpec as P

TILE = 128
SIZES = {"y": 4, "z": 8, "x": 4, "core": 2}
ROW = ("y", "z")
COL = ("x", "core")
VM = pltpu.VMEM
F32 = jnp.float32
BF16 = jnp.bfloat16
STEPS = (0, 1, 2, -1)


def from_ahead(value, axis, k):
    n = SIZES[axis]
    return lax.ppermute(value, axis, [((i + k) % n, i) for i in range(n)])


def to_ahead(value, axis, k):
    n = SIZES[axis]
    return lax.ppermute(value, axis, [(i, (i + k) % n) for i in range(n)])


def call(body, outs, smem, vmem, flops=0, scratch=(), limit=24):
    outs = [jax.ShapeDtypeStruct(s, d) for s, d in outs]
    return pl.pallas_call(
        body,
        out_shape=outs,
        in_specs=[pl.BlockSpec(memory_space=pltpu.SMEM)] * len(smem)
        + [pl.BlockSpec(memory_space=VM)] * len(vmem),
        out_specs=[pl.BlockSpec(memory_space=VM)] * len(outs),
        scratch_shapes=list(scratch),
        compiler_params=pltpu.CompilerParams(vmem_limit_bytes=limit * 2**20),
        cost_estimate=pl.CostEstimate(
            flops=flops,
            transcendentals=0,
            bytes_accessed=sum(v.size * v.dtype.itemsize for v in vmem)
            + sum(o.size * o.dtype.itemsize for o in outs),
        ),
    )(*smem, *vmem)


def tile_ref(ref, r, c):
    return ref.at[
        pl.ds(pl.multiple_of(r * TILE, TILE), TILE), pl.ds(pl.multiple_of(c * TILE, TILE), TILE)
    ]


def mask_body(rows, cols, count, w, out, flipped):
    out[...] = jnp.zeros_like(out)
    flipped[...] = jnp.zeros_like(flipped)

    @pl.loop(0, count[0])
    def _(k):
        tile = tile_ref(w, rows[k], cols[k])[...]
        tile_ref(out, rows[k], cols[k])[...] = tile
        tile_ref(flipped, cols[k], rows[k])[...] = tile.T


def zpos(pos, i, hi):
    return (pos[1] + i + 4 * hi + 8) % 8


def z_step(i, j):
    return -2 if i == 2 and j >= 2 else STEPS[i]


def at_step(pieces, step, k):
    if step == 2:
        return pieces[2 + k // 2], k % 2
    return pieces[step + step // 3], k


def up_body(pos, *refs):
    a3, b3, w = refs[:5], refs[5:10], refs[10]
    keep, send, toks, acc = refs[11:]
    core = pos[3]
    cut = a3[0].shape[-1]
    back = pos[0] - pos[2] + 4
    for j in range(4):
        d = (j + back) % 4
        for i in range(4):
            a_ref, a_at = at_step(a3, i, j)
            b_ref, b_at = at_step(b3, j, i)

            @pl.loop(0, 2)
            def _(hi, i=i, j=j, d=d, a_ref=a_ref, a_at=a_at, b_ref=b_ref, b_at=b_at):
                at = zpos(pos, STEPS[i], hi)
                low = zpos(pos, z_step(i, j), hi)
                toks[d, low, :, :cut] = a_ref[a_at, hi]
                toks[d, at, :, cut:] = b_ref[b_at, hi]

    @pl.loop(0, 4)
    def _(d):
        part = jnp.dot(
            toks[d].reshape(-1, toks.shape[-1]), w[...], preferred_element_type=F32
        )
        acc[...] = part.reshape(acc.shape)
        keep[d] = acc[core]
        send[d] = acc[1 - core].astype(BF16)


def collect(pos, mine, other, slots, sems):
    core = pos[3]
    copies = [
        pltpu.make_async_copy(g, slots(side), sems.at[s])
        for s, (side, g) in enumerate(((core, mine), (1 - core, other)))
    ]
    for c in copies:
        c.start()
    for c in copies:
        c.wait()


def back_first_body(pos, *refs):
    mine, other, w, total, grads, sems = refs
    collect(pos, mine, other, lambda side: grads.at[:, side], sems)

    @pl.loop(0, 4)
    def _(d):
        g = grads[d].reshape(-1, grads.shape[-1])
        part = jnp.dot(g, w[: g.shape[1]], preferred_element_type=F32)
        total[d] = part.reshape(total.shape[1:])


def back_second_body(pos, *refs):
    mine, other, w, total, first = refs[:5]
    a3, b3, grads = refs[5:9], refs[9:13], refs[13]
    acc, sems, first_sem = refs[14:]
    cut = first.shape[-1]
    kept = pltpu.make_async_copy(first, grads.at[:, :, :, pl.ds(0, cut)], first_sem)
    kept.start()
    collect(pos, mine, other, lambda side: grads.at[:, side, :, pl.ds(cut, cut)], sems)
    back = pos[0] - pos[2] + 4

    @pl.loop(0, 4)
    def _(j):
        d = (j + back) % 4
        g = grads[d, :, :, cut:].reshape(-1, cut)
        part = jnp.dot(g, w[cut:], preferred_element_type=F32)
        acc[j] = total[d] + part.reshape(total.shape[1:])

    kept.wait()
    cut = a3[0].shape[-1]
    for hi in range(2):
        for k in range(4):

            @pl.loop(0, 4)
            def _(j, k=k, hi=hi):
                step = jnp.where(j >= 2, z_step(k, 2), z_step(k, 0))
                piece = acc[j, zpos(pos, step, hi), :, :cut]
                a3[k][j, hi] = piece.astype(a3[k].dtype)

            @pl.loop(0, 4)
            def _(i, k=k, hi=hi):
                piece = acc[k, zpos(pos, jnp.where(i == 3, -1, i), hi), :, cut:]
                b3[k][i, hi] = piece.astype(b3[k].dtype)


def add_body(keep, recv, *out):
    for d in range(4):

        @pl.loop(0, keep.shape[1] // 16)
        def _(i, d=d):
            at = pl.ds(pl.multiple_of(i * 16, 16), 16)
            total = keep[d, at] + recv[d, at].astype(F32)
            out[d][at] = total.astype(out[d].dtype)


def act_body(own, r1, r2, r3, cot, hidden, *grads):
    step = grads[0].shape[1]

    @pl.loop(0, own.shape[0] // 16)
    def _(i):
        rows = pl.ds(pl.multiple_of(i * 16, 16), 16)
        for k, grad_pre in enumerate(grads):
            at = (rows, slice(k * step, (k + 1) * step))
            pre_act = own[at] + r1[at].astype(F32) + r2[at].astype(F32) + r3[at].astype(F32)
            gate = jax.nn.sigmoid(pre_act)
            hidden[at] = (pre_act * gate).astype(BF16)
            slope = gate * (1.0 + pre_act * (1.0 - gate))
            grad_pre[rows] = (cot[at].astype(F32) * slope).astype(BF16)


def wgrad_body(rows, cols, count, toks, grads, out, acc):
    acc[...] = jnp.zeros_like(acc)
    step = 512

    @pl.loop(0, 4)
    def _(d):
        t = toks[d].reshape(-1, toks.shape[-1])

        @pl.loop(0, acc.shape[1] // step)
        def _(k):
            at = pl.ds(pl.multiple_of(k * step, step), step)
            g = grads[d, :, :, at].reshape(-1, step)
            acc[:, at] += lax.dot_general(
                t, g, (((0,), (0,)), ((), ())), preferred_element_type=F32
            )

    out[...] = jnp.zeros_like(out)

    @pl.loop(0, count[0])
    def _(k):
        tile_ref(out, rows[k], cols[k])[...] = tile_ref(acc, rows[k], cols[k])[...].astype(BF16)


def gather_four(piece, axis):
    return [piece] + [from_ahead(piece, axis, k) for k in STEPS[1:]]


def ring_gather(piece, axis):
    ahead, behind = from_ahead(piece, axis, 1), from_ahead(piece, axis, -1)
    half = piece.shape[0] // 2
    far = [from_ahead(ahead[:half], axis, 1), from_ahead(behind[half:], axis, -1)]
    return [piece, ahead] + far + [behind]


def gather_tokens(tokens):
    pair = jnp.stack([tokens, from_ahead(tokens, "z", 4)])
    cut = tokens.shape[1] // 2
    a2 = gather_four(pair[:, :, :cut], "y")
    b2 = gather_four(pair[:, :, cut:], "z")
    a2, b2 = lax.optimization_barrier((a2, b2))
    return ring_gather(jnp.stack(a2), "z"), ring_gather(jnp.stack(b2), "y")


def activation(keep, recv, cot):
    shape = keep.shape[1:]
    own, *sends = call(add_body, [(shape, F32)] + [(shape, BF16)] * 3, [], [keep, recv])
    recvs = [to_ahead(s, "x", d + 1) for d, s in enumerate(sends)]
    cut = shape[1] // 2
    outs = [(shape, BF16)] + [((shape[0], cut), BF16)] * 2
    return call(act_body, outs, [], [own] + recvs + [cot])


def gather_grads(grad_pre):
    mine = jnp.stack([grad_pre] + [from_ahead(grad_pre, "x", d) for d in range(1, 4)])
    return [mine, to_ahead(mine, "core", 1)]


def reduce_four(own, sends, axis):
    total = own
    for k, s in zip(STEPS[1:], sends):
        total = total + to_ahead(s.astype(BF16), axis, k).astype(F32)
    return total


def ring_reduce(own, ahead, far, behind, axis):
    half = own.shape[0] // 2
    lo = to_ahead(far[:half], axis, 1).astype(F32)
    hi = to_ahead(far[half:], axis, -1).astype(F32)
    ahead = jnp.concatenate([ahead[:half] + lo, ahead[half:]])
    behind = jnp.concatenate([behind[:half], behind[half:] + hi])
    total = own + to_ahead(ahead.astype(BF16), axis, 1).astype(F32)
    return total + to_ahead(behind.astype(BF16), axis, -1).astype(F32)


def middle(a3, b3, wm, flipped, pos, cot):
    rows = a3[0].shape[2] * 4
    depth, width = wm.shape
    cut = width // 2
    flops = 8 * rows * depth * width
    keep, send, toks = call(
        up_body,
        [
            ((4, rows, width), F32),
            ((4, rows, width), BF16),
            ((4, 8, rows // 4, depth), BF16),
        ],
        [pos],
        a3 + b3 + [wm],
        2 * flops,
        [VM((2, rows, width), F32)],
    )
    recv = to_ahead(send, "core", 1)
    hidden, grad1, grad2 = activation(keep, recv, cot)
    parts1 = gather_grads(grad1)
    parts2 = gather_grads(grad2)
    g_shape = ((4, 2, rows, cut), BF16)
    sems = pltpu.SemaphoreType.DMA((2,))
    sums = (4, 8, rows // 4, depth)
    total, g1 = call(
        back_first_body, [(sums, F32), g_shape], [pos], parts1 + [flipped], flops, [sems]
    )
    shape = (4, 2, rows // 4, depth // 2)
    outs = [(shape, d) for d in (F32, F32, BF16, F32)]
    *sends, grads = call(
        back_second_body,
        outs + outs + [((4, 2, rows, width), BF16)],
        [pos],
        parts2 + [flipped, total, g1],
        flops,
        [VM(sums, F32), sems, pltpu.SemaphoreType.DMA],
    )
    return hidden, sends, toks, grads


def reduce_inputs(sends, weight_grad):
    a2 = ring_reduce(*sends[:4], "z")
    b2 = ring_reduce(*sends[4:], "y")
    a2, b2, weight_grad = lax.optimization_barrier((a2, b2, weight_grad))
    a1 = reduce_four(a2[0], a2[1:], "y")
    b1 = reduce_four(b2[0], b2[1:], "z")
    both = jnp.concatenate([a1, b1], axis=-1)
    total = both[0] + to_ahead(both[1].astype(BF16), "z", 4).astype(F32)
    return total.astype(BF16), weight_grad


def on_device(tokens, weight, tile_rows, tile_cols, tile_count, hidden_cotangent):
    y, z, x, core = (lax.axis_index(a) for a in ("y", "z", "x", "core"))
    pos = jnp.stack([y, z, x, core]).astype(jnp.int32)
    row_blocks = weight.shape[0] // TILE
    col_blocks = weight.shape[1] // TILE
    rows = tile_rows.reshape(-1) - (x * 2 + core) * row_blocks
    cols = tile_cols.reshape(-1) - (y * 8 + z) * col_blocks
    count = tile_count.reshape(1)
    shapes = [(weight.shape, BF16), (weight.shape[::-1], BF16)]
    wm, flipped = call(mask_body, shapes, [rows, cols, count], [weight])
    a3, b3 = gather_tokens(tokens)
    hidden, sends, toks, grads = middle(a3, b3, wm, flipped, pos, hidden_cotangent)
    (weight_grad,) = call(
        wgrad_body,
        [(weight.shape, BF16)],
        [rows, cols, count],
        [toks, grads],
        2 * 1536 * weight.size,
        [VM(weight.shape, F32)],
    )
    input_grad, weight_grad = reduce_inputs(sends, weight_grad)
    return hidden, input_grad, weight_grad


def solution(mesh):
    split = Mesh(mesh.devices.reshape(4, 8, 4, 2), ("y", "z", "x", "core"))
    return jax.shard_map(
        on_device,
        mesh=split,
        in_specs=(
            P(ROW, COL),
            P(COL, ROW),
            P(ROW, COL, None),
            P(ROW, COL, None),
            P(ROW, COL),
            P(COL, ROW),
        ),
        out_specs=(P(COL, ROW), P(ROW, COL), P(COL, ROW)),
        check_vma=False,
    )
```

```python
import functools

import jax
import jax.numpy as jnp
from jax import lax
from jax.experimental import pallas as pl
from jax.experimental.pallas import tpu as pltpu
from jax.sharding import Mesh
from jax.sharding import PartitionSpec as P

TILE = 128
SIZES = {"y": 4, "z": 8, "x": 4, "core": 2}
ROW = ("y", "z")
COL = ("x", "core")
VM = pltpu.VMEM
F32 = jnp.float32
BF16 = jnp.bfloat16
STEPS = (0, 1, 2, -1)


def from_ahead(value, axis, k):
    n = SIZES[axis]
    return lax.ppermute(value, axis, [((i + k) % n, i) for i in range(n)])


def to_ahead(value, axis, k):
    n = SIZES[axis]
    return lax.ppermute(value, axis, [(i, (i + k) % n) for i in range(n)])


def call(body, outs, smem, vmem, flops=0, scratch=(), limit=24):
    outs = [jax.ShapeDtypeStruct(s, d) for s, d in outs]
    return pl.pallas_call(
        body,
        out_shape=outs,
        in_specs=[pl.BlockSpec(memory_space=pltpu.SMEM)] * len(smem)
        + [pl.BlockSpec(memory_space=VM)] * len(vmem),
        out_specs=[pl.BlockSpec(memory_space=VM)] * len(outs),
        scratch_shapes=list(scratch),
        compiler_params=pltpu.CompilerParams(vmem_limit_bytes=limit * 2**20),
        cost_estimate=pl.CostEstimate(
            flops=flops,
            transcendentals=0,
            bytes_accessed=sum(v.size * v.dtype.itemsize for v in vmem)
            + sum(o.size * o.dtype.itemsize for o in outs),
        ),
    )(*smem, *vmem)


def tile_ref(ref, r, c):
    return ref.at[
        pl.ds(pl.multiple_of(r * TILE, TILE), TILE), pl.ds(pl.multiple_of(c * TILE, TILE), TILE)
    ]


def mask_body(rows, cols, count, w, out, flipped):
    out[...] = jnp.zeros_like(out)
    flipped[...] = jnp.zeros_like(flipped)

    @pl.loop(0, count[0])
    def _(k):
        tile = tile_ref(w, rows[k], cols[k])[...]
        tile_ref(out, rows[k], cols[k])[...] = tile
        tile_ref(flipped, cols[k], rows[k])[...] = tile.T


def zpos(pos, i, hi):
    return (pos[1] + i + 4 * hi + 8) % 8


def up_body(pos, *refs):
    a3, b3, w = refs[:4], refs[4:8], refs[8]
    keep, send, toks, acc = refs[9:]
    core = pos[3]
    cut = a3[0].shape[-1]
    back = pos[0] - pos[2] + 4
    for j in range(4):
        d = (j + back) % 4
        for i in range(4):

            @pl.loop(0, 2)
            def _(hi, i=i, j=j, d=d):
                at = zpos(pos, STEPS[i], hi)
                toks[d, at, :, :cut] = a3[i][j, hi]
                toks[d, at, :, cut:] = b3[j][i, hi]

    @pl.loop(0, 4)
    def _(d):
        part = jnp.dot(
            toks[d].reshape(-1, toks.shape[-1]), w[...], preferred_element_type=F32
        )
        acc[...] = part.reshape(acc.shape)
        keep[d] = acc[core]
        send[d] = acc[1 - core].astype(BF16)


def collect(pos, mine, other, slots, sems):
    core = pos[3]
    copies = [
        pltpu.make_async_copy(g, slots(side), sems.at[s])
        for s, (side, g) in enumerate(((core, mine), (1 - core, other)))
    ]
    for c in copies:
        c.start()
    for c in copies:
        c.wait()


def back_first_body(pos, *refs):
    mine, other, w, total, grads, sems = refs
    collect(pos, mine, other, lambda side: grads.at[:, side], sems)

    @pl.loop(0, 4)
    def _(d):
        g = grads[d].reshape(-1, grads.shape[-1])
        part = jnp.dot(g, w[: g.shape[1]], preferred_element_type=F32)
        total[d] = part.reshape(total.shape[1:])


def back_second_body(pos, *refs):
    mine, other, w, total, first = refs[:5]
    a3, b3, grads = refs[5:9], refs[9:13], refs[13]
    acc, sems, first_sem = refs[14:]
    cut = first.shape[-1]
    kept = pltpu.make_async_copy(first, grads.at[:, :, :, pl.ds(0, cut)], first_sem)
    kept.start()
    collect(pos, mine, other, lambda side: grads.at[:, side, :, pl.ds(cut, cut)], sems)
    back = pos[0] - pos[2] + 4

    @pl.loop(0, 4)
    def _(j):
        d = (j + back) % 4
        g = grads[d, :, :, cut:].reshape(-1, cut)
        part = jnp.dot(g, w[cut:], preferred_element_type=F32)
        acc[j] = total[d] + part.reshape(total.shape[1:])

    kept.wait()
    cut = a3[0].shape[-1]
    for hi in range(2):
        for k in range(4):

            @pl.loop(0, 4)
            def _(j, k=k, hi=hi):
                piece = acc[j, zpos(pos, STEPS[k], hi), :, :cut]
                a3[k][j, hi] = piece.astype(a3[k].dtype)

            @pl.loop(0, 4)
            def _(i, k=k, hi=hi):
                piece = acc[k, zpos(pos, jnp.where(i == 3, -1, i), hi), :, cut:]
                b3[k][i, hi] = piece.astype(b3[k].dtype)


def add_body(cols, keep, recv, *out):
    for d in range(4):

        @pl.loop(0, keep.shape[1] // 16)
        def _(i, d=d):
            at = pl.ds(pl.multiple_of(i * 16, 16), 16)
            total = keep[d, at, cols] + recv[d, at, cols].astype(F32)
            out[d][at] = total.astype(out[d].dtype)


def act_body(cols, own, r1, r2, r3, cot, hidden, grad_pre):
    @pl.loop(0, own.shape[0] // 16)
    def _(i):
        at = pl.ds(pl.multiple_of(i * 16, 16), 16)
        pre_act = own[at] + r1[at].astype(F32) + r2[at].astype(F32) + r3[at].astype(F32)
        gate = jax.nn.sigmoid(pre_act)
        hidden[at] = (pre_act * gate).astype(BF16)
        slope = gate * (1.0 + pre_act * (1.0 - gate))
        grad_pre[at] = (cot[at, cols].astype(F32) * slope).astype(BF16)


def wgrad_body(rows, cols, count, toks, grads, out, acc):
    acc[...] = jnp.zeros_like(acc)
    step = 512

    @pl.loop(0, 4)
    def _(d):
        t = toks[d].reshape(-1, toks.shape[-1])

        @pl.loop(0, acc.shape[1] // step)
        def _(k):
            at = pl.ds(pl.multiple_of(k * step, step), step)
            g = grads[d, :, :, at].reshape(-1, step)
            acc[:, at] += lax.dot_general(
                t, g, (((0,), (0,)), ((), ())), preferred_element_type=F32
            )

    out[...] = jnp.zeros_like(out)

    @pl.loop(0, count[0])
    def _(k):
        tile_ref(out, rows[k], cols[k])[...] = tile_ref(acc, rows[k], cols[k])[...].astype(BF16)


def gather_four(piece, axis):
    return [piece] + [from_ahead(piece, axis, k) for k in STEPS[1:]]


def ring_gather(piece, axis):
    ahead = from_ahead(piece, axis, 1)
    behind = from_ahead(piece, axis, -1)
    return [piece, ahead, from_ahead(ahead, axis, 1), behind]


def gather_tokens(tokens):
    pair = jnp.stack([tokens, from_ahead(tokens, "z", 4)])
    cut = tokens.shape[1] // 2
    a2 = gather_four(pair[:, :, :cut], "y")
    b2 = gather_four(pair[:, :, cut:], "z")
    a2, b2 = lax.optimization_barrier((a2, b2))
    return ring_gather(jnp.stack(a2), "z"), ring_gather(jnp.stack(b2), "y")


def partial_sums(keep, recv, cols):
    shape = (keep.shape[1], cols.stop - cols.start)
    body = functools.partial(add_body, cols)
    return call(body, [(shape, F32)] + [(shape, BF16)] * 3, [], [keep, recv])


def activation(own, sends, cot, cols):
    recvs = [to_ahead(s, "x", d + 1) for d, s in enumerate(sends)]
    body = functools.partial(act_body, cols)
    return call(body, [(own.shape, BF16)] * 2, [], [own] + recvs + [cot])


def gather_grads(grad_pre):
    mine = jnp.stack([grad_pre] + [from_ahead(grad_pre, "x", d) for d in range(1, 4)])
    return [mine, to_ahead(mine, "core", 1)]


def reduce_four(own, sends, axis):
    total = own
    for k, s in zip(STEPS[1:], sends):
        total = total + to_ahead(s.astype(BF16), axis, k).astype(F32)
    return total


def ring_reduce(own, ahead, far, behind, axis):
    through = to_ahead(far, axis, 1).astype(F32)
    total = own + to_ahead(behind, axis, -1).astype(F32)
    return total + to_ahead((ahead + through).astype(BF16), axis, 1).astype(F32)


def middle(a3, b3, wm, flipped, pos, cot):
    rows = a3[0].shape[2] * 4
    depth, width = wm.shape
    cut = width // 2
    flops = 8 * rows * depth * width
    keep, send, toks = call(
        up_body,
        [
            ((4, rows, width), F32),
            ((4, rows, width), BF16),
            ((4, 8, rows // 4, depth), BF16),
        ],
        [pos],
        a3 + b3 + [wm],
        2 * flops,
        [VM((2, rows, width), F32)],
    )
    recv = to_ahead(send, "core", 1)
    cols1, cols2 = slice(0, cut), slice(cut, width)
    own1, *sends1 = partial_sums(keep, recv, cols1)
    own2, *sends2 = partial_sums(keep, recv, cols2)
    hidden1, grad1 = activation(own1, sends1, cot, cols1)
    hidden2, grad2 = activation(own2, sends2, cot, cols2)
    hidden = jnp.concatenate([hidden1, hidden2], axis=1)
    parts1 = gather_grads(grad1)
    parts2 = gather_grads(grad2)
    g_shape = ((4, 2, rows, cut), BF16)
    sems = pltpu.SemaphoreType.DMA((2,))
    sums = (4, 8, rows // 4, depth)
    total, g1 = call(
        back_first_body, [(sums, F32), g_shape], [pos], parts1 + [flipped], flops, [sems]
    )
    shape = (4, 2, rows // 4, depth // 2)
    outs = [(shape, d) for d in (F32, F32, BF16, BF16)]
    *sends, grads = call(
        back_second_body,
        outs + outs + [((4, 2, rows, width), BF16)],
        [pos],
        parts2 + [flipped, total, g1],
        flops,
        [VM(sums, F32), sems, pltpu.SemaphoreType.DMA],
    )
    return hidden, sends, toks, grads


def reduce_inputs(sends, weight_grad):
    a2 = ring_reduce(*sends[:4], "z")
    b2 = ring_reduce(*sends[4:], "y")
    a2, b2, weight_grad = lax.optimization_barrier((a2, b2, weight_grad))
    a1 = reduce_four(a2[0], a2[1:], "y")
    b1 = reduce_four(b2[0], b2[1:], "z")
    both = jnp.concatenate([a1, b1], axis=-1)
    total = both[0] + to_ahead(both[1].astype(BF16), "z", 4).astype(F32)
    return total.astype(BF16), weight_grad


def on_device(tokens, weight, tile_rows, tile_cols, tile_count, hidden_cotangent):
    y, z, x, core = (lax.axis_index(a) for a in ("y", "z", "x", "core"))
    pos = jnp.stack([y, z, x, core]).astype(jnp.int32)
    row_blocks = weight.shape[0] // TILE
    col_blocks = weight.shape[1] // TILE
    rows = tile_rows.reshape(-1) - (x * 2 + core) * row_blocks
    cols = tile_cols.reshape(-1) - (y * 8 + z) * col_blocks
    count = tile_count.reshape(1)
    shapes = [(weight.shape, BF16), (weight.shape[::-1], BF16)]
    wm, flipped = call(mask_body, shapes, [rows, cols, count], [weight])
    a3, b3 = gather_tokens(tokens)
    hidden, sends, toks, grads = middle(a3, b3, wm, flipped, pos, hidden_cotangent)
    (weight_grad,) = call(
        wgrad_body,
        [(weight.shape, BF16)],
        [rows, cols, count],
        [toks, grads],
        2 * 1536 * weight.size,
        [VM(weight.shape, F32)],
    )
    input_grad, weight_grad = reduce_inputs(sends, weight_grad)
    return hidden, input_grad, weight_grad


def solution(mesh):
    split = Mesh(mesh.devices.reshape(4, 8, 4, 2), ("y", "z", "x", "core"))
    return jax.shard_map(
        on_device,
        mesh=split,
        in_specs=(
            P(ROW, COL),
            P(COL, ROW),
            P(ROW, COL, None),
            P(ROW, COL, None),
            P(ROW, COL),
            P(COL, ROW),
        ),
        out_specs=(P(COL, ROW), P(ROW, COL), P(COL, ROW)),
        check_vma=False,
    )
```

```python
import functools

import jax
import jax.numpy as jnp
from jax import lax
from jax.experimental import pallas as pl
from jax.experimental.pallas import tpu as pltpu
from jax.sharding import Mesh
from jax.sharding import PartitionSpec as P

TILE = 128
SIZES = {"y": 4, "z": 8, "x": 4, "core": 2}
ROW = ("y", "z")
COL = ("x", "core")
VM = pltpu.VMEM
F32 = jnp.float32
BF16 = jnp.bfloat16
STEPS = (0, 1, 2, -1)


def from_ahead(value, axis, k):
    n = SIZES[axis]
    return lax.ppermute(value, axis, [((i + k) % n, i) for i in range(n)])


def to_ahead(value, axis, k):
    n = SIZES[axis]
    return lax.ppermute(value, axis, [(i, (i + k) % n) for i in range(n)])


def call(body, outs, smem, vmem, flops=0, scratch=(), limit=24):
    outs = [jax.ShapeDtypeStruct(s, d) for s, d in outs]
    return pl.pallas_call(
        body,
        out_shape=outs,
        in_specs=[pl.BlockSpec(memory_space=pltpu.SMEM)] * len(smem)
        + [pl.BlockSpec(memory_space=VM)] * len(vmem),
        out_specs=[pl.BlockSpec(memory_space=VM)] * len(outs),
        scratch_shapes=list(scratch),
        compiler_params=pltpu.CompilerParams(vmem_limit_bytes=limit * 2**20),
        cost_estimate=pl.CostEstimate(
            flops=flops,
            transcendentals=0,
            bytes_accessed=sum(v.size * v.dtype.itemsize for v in vmem)
            + sum(o.size * o.dtype.itemsize for o in outs),
        ),
    )(*smem, *vmem)


def tile_ref(ref, r, c):
    return ref.at[
        pl.ds(pl.multiple_of(r * TILE, TILE), TILE), pl.ds(pl.multiple_of(c * TILE, TILE), TILE)
    ]


def mask_body(rows, cols, count, w, out, flipped):
    out[...] = jnp.zeros_like(out)
    flipped[...] = jnp.zeros_like(flipped)

    @pl.loop(0, count[0])
    def _(k):
        tile = tile_ref(w, rows[k], cols[k])[...]
        tile_ref(out, rows[k], cols[k])[...] = tile
        tile_ref(flipped, cols[k], rows[k])[...] = tile.T


def zpos(pos, i, hi):
    return (pos[1] + i + 4 * hi + 8) % 8


def up_body(pos, *refs):
    a3, b3, w = refs[:4], refs[4:8], refs[8]
    keep, send, toks, acc = refs[9:]
    core = pos[3]
    cut = a3[0].shape[-1]
    back = pos[0] - pos[2] + 4
    for j in range(4):
        d = (j + back) % 4
        for i in range(4):

            @pl.loop(0, 2)
            def _(hi, i=i, j=j, d=d):
                at = zpos(pos, STEPS[i], hi)
                toks[d, at, :, :cut] = a3[i][j, hi]
                toks[d, at, :, cut:] = b3[j][i, hi]

    @pl.loop(0, 4)
    def _(d):
        part = jnp.dot(
            toks[d].reshape(-1, toks.shape[-1]), w[...], preferred_element_type=F32
        )
        acc[...] = part.reshape(acc.shape)
        keep[d] = acc[core]
        send[d] = acc[1 - core].astype(BF16)


def collect(pos, mine, other, slots, sems):
    core = pos[3]
    copies = [
        pltpu.make_async_copy(g, slots(side), sems.at[s])
        for s, (side, g) in enumerate(((core, mine), (1 - core, other)))
    ]
    for c in copies:
        c.start()
    for c in copies:
        c.wait()


def back_first_body(pos, *refs):
    mine, other, w, total, grads, sems = refs
    collect(pos, mine, other, lambda side: grads.at[:, side], sems)

    @pl.loop(0, 4)
    def _(d):
        g = grads[d].reshape(-1, grads.shape[-1])
        part = jnp.dot(g, w[: g.shape[1]], preferred_element_type=F32)
        total[d] = part.reshape(total.shape[1:])


def back_second_body(pos, *refs):
    mine, other, w, total, first = refs[:5]
    a3, b3, grads = refs[5:9], refs[9:13], refs[13]
    acc, sems, first_sem = refs[14:]
    cut = first.shape[-1]
    kept = pltpu.make_async_copy(first, grads.at[:, :, :, pl.ds(0, cut)], first_sem)
    kept.start()
    collect(pos, mine, other, lambda side: grads.at[:, side, :, pl.ds(cut, cut)], sems)
    back = pos[0] - pos[2] + 4

    @pl.loop(0, 4)
    def _(j):
        d = (j + back) % 4
        g = grads[d, :, :, cut:].reshape(-1, cut)
        part = jnp.dot(g, w[cut:], preferred_element_type=F32)
        acc[j] = total[d] + part.reshape(total.shape[1:])

    kept.wait()
    cut = a3[0].shape[-1]
    for hi in range(2):
        for k in range(4):

            @pl.loop(0, 4)
            def _(j, k=k, hi=hi):
                piece = acc[j, zpos(pos, STEPS[k], hi), :, :cut]
                a3[k][j, hi] = piece.astype(a3[k].dtype)

            @pl.loop(0, 4)
            def _(i, k=k, hi=hi):
                piece = acc[k, zpos(pos, jnp.where(i == 3, -1, i), hi), :, cut:]
                b3[k][i, hi] = piece.astype(b3[k].dtype)


def add_body(cols, keep, recv, *out):
    for d in range(4):

        @pl.loop(0, keep.shape[1] // 16)
        def _(i, d=d):
            at = pl.ds(pl.multiple_of(i * 16, 16), 16)
            total = keep[d, at, cols] + recv[d, at, cols].astype(F32)
            out[d][at] = total.astype(out[d].dtype)


def act_body(cols, own, r1, r2, r3, cot, hidden, grad_pre):
    @pl.loop(0, own.shape[0] // 16)
    def _(i):
        at = pl.ds(pl.multiple_of(i * 16, 16), 16)
        pre_act = own[at] + r1[at].astype(F32) + r2[at].astype(F32) + r3[at].astype(F32)
        gate = jax.nn.sigmoid(pre_act)
        hidden[at] = (pre_act * gate).astype(BF16)
        slope = gate * (1.0 + pre_act * (1.0 - gate))
        grad_pre[at] = (cot[at, cols].astype(F32) * slope).astype(BF16)


def wgrad_body(rows, cols, count, toks, grads, out, acc):
    acc[...] = jnp.zeros_like(acc)
    step = 512

    @pl.loop(0, 4)
    def _(d):
        t = toks[d].reshape(-1, toks.shape[-1])

        @pl.loop(0, acc.shape[1] // step)
        def _(k):
            at = pl.ds(pl.multiple_of(k * step, step), step)
            g = grads[d, :, :, at].reshape(-1, step)
            acc[:, at] += lax.dot_general(
                t, g, (((0,), (0,)), ((), ())), preferred_element_type=F32
            )

    out[...] = jnp.zeros_like(out)

    @pl.loop(0, count[0])
    def _(k):
        tile_ref(out, rows[k], cols[k])[...] = tile_ref(acc, rows[k], cols[k])[...].astype(BF16)


def ring_gather(piece, axis):
    ahead = from_ahead(piece, axis, 1)
    behind = from_ahead(piece, axis, -1)
    return [piece, ahead, from_ahead(ahead, axis, 1), behind]


def gather_tokens(tokens):
    pair = jnp.stack([tokens, from_ahead(tokens, "z", 4)])
    cut = tokens.shape[1] // 2
    a2 = ring_gather(pair[:, :, :cut], "y")
    b2 = ring_gather(pair[:, :, cut:], "z")
    a2, b2 = lax.optimization_barrier((a2, b2))
    return ring_gather(jnp.stack(a2), "z"), ring_gather(jnp.stack(b2), "y")


def partial_sums(keep, recv, cols):
    shape = (keep.shape[1], cols.stop - cols.start)
    body = functools.partial(add_body, cols)
    return call(body, [(shape, F32)] + [(shape, BF16)] * 3, [], [keep, recv])


def activation(own, sends, cot, cols):
    recvs = [to_ahead(s, "x", d + 1) for d, s in enumerate(sends)]
    body = functools.partial(act_body, cols)
    return call(body, [(own.shape, BF16)] * 2, [], [own] + recvs + [cot])


def gather_grads(grad_pre):
    mine = jnp.stack([grad_pre] + [from_ahead(grad_pre, "x", d) for d in range(1, 4)])
    return [mine, to_ahead(mine, "core", 1)]


def ring_reduce(own, ahead, far, behind, axis):
    through = to_ahead(far.astype(BF16), axis, 1).astype(F32)
    total = own + to_ahead(behind.astype(BF16), axis, -1).astype(F32)
    return total + to_ahead((ahead + through).astype(BF16), axis, 1).astype(F32)


def middle(a3, b3, wm, flipped, pos, cot):
    rows = a3[0].shape[2] * 4
    depth, width = wm.shape
    cut = width // 2
    flops = 8 * rows * depth * width
    keep, send, toks = call(
        up_body,
        [
            ((4, rows, width), F32),
            ((4, rows, width), BF16),
            ((4, 8, rows // 4, depth), BF16),
        ],
        [pos],
        a3 + b3 + [wm],
        2 * flops,
        [VM((2, rows, width), F32)],
    )
    recv = to_ahead(send, "core", 1)
    cols1, cols2 = slice(0, cut), slice(cut, width)
    own1, *sends1 = partial_sums(keep, recv, cols1)
    own2, *sends2 = partial_sums(keep, recv, cols2)
    hidden1, grad1 = activation(own1, sends1, cot, cols1)
    hidden2, grad2 = activation(own2, sends2, cot, cols2)
    hidden = jnp.concatenate([hidden1, hidden2], axis=1)
    parts1 = gather_grads(grad1)
    parts2 = gather_grads(grad2)
    g_shape = ((4, 2, rows, cut), BF16)
    sems = pltpu.SemaphoreType.DMA((2,))
    sums = (4, 8, rows // 4, depth)
    total, g1 = call(
        back_first_body, [(sums, F32), g_shape], [pos], parts1 + [flipped], flops, [sems]
    )
    shape = (4, 2, rows // 4, depth // 2)
    outs = [(shape, d) for d in (F32, F32, BF16, BF16)]
    *sends, grads = call(
        back_second_body,
        outs + outs + [((4, 2, rows, width), BF16)],
        [pos],
        parts2 + [flipped, total, g1],
        flops,
        [VM(sums, F32), sems, pltpu.SemaphoreType.DMA],
    )
    return hidden, sends, toks, grads


def reduce_inputs(sends, weight_grad):
    a2 = ring_reduce(*sends[:4], "z")
    b2 = ring_reduce(*sends[4:], "y")
    a2, b2, weight_grad = lax.optimization_barrier((a2, b2, weight_grad))
    a1 = ring_reduce(*a2, "y")
    b1 = ring_reduce(*b2, "z")
    both = jnp.concatenate([a1, b1], axis=-1)
    total = both[0] + to_ahead(both[1].astype(BF16), "z", 4).astype(F32)
    return total.astype(BF16), weight_grad


def on_device(tokens, weight, tile_rows, tile_cols, tile_count, hidden_cotangent):
    y, z, x, core = (lax.axis_index(a) for a in ("y", "z", "x", "core"))
    pos = jnp.stack([y, z, x, core]).astype(jnp.int32)
    row_blocks = weight.shape[0] // TILE
    col_blocks = weight.shape[1] // TILE
    rows = tile_rows.reshape(-1) - (x * 2 + core) * row_blocks
    cols = tile_cols.reshape(-1) - (y * 8 + z) * col_blocks
    count = tile_count.reshape(1)
    shapes = [(weight.shape, BF16), (weight.shape[::-1], BF16)]
    wm, flipped = call(mask_body, shapes, [rows, cols, count], [weight])
    a3, b3 = gather_tokens(tokens)
    hidden, sends, toks, grads = middle(a3, b3, wm, flipped, pos, hidden_cotangent)
    (weight_grad,) = call(
        wgrad_body,
        [(weight.shape, BF16)],
        [rows, cols, count],
        [toks, grads],
        2 * 1536 * weight.size,
        [VM(weight.shape, F32)],
    )
    input_grad, weight_grad = reduce_inputs(sends, weight_grad)
    return hidden, input_grad, weight_grad


def solution(mesh):
    split = Mesh(mesh.devices.reshape(4, 8, 4, 2), ("y", "z", "x", "core"))
    return jax.shard_map(
        on_device,
        mesh=split,
        in_specs=(
            P(ROW, COL),
            P(COL, ROW),
            P(ROW, COL, None),
            P(ROW, COL, None),
            P(ROW, COL),
            P(COL, ROW),
        ),
        out_specs=(P(COL, ROW), P(ROW, COL), P(COL, ROW)),
        check_vma=False,
    )
```

```python
import functools

import jax
import jax.numpy as jnp
from jax import lax
from jax.experimental import pallas as pl
from jax.experimental.pallas import tpu as pltpu
from jax.sharding import Mesh
from jax.sharding import PartitionSpec as P

TILE = 128
SIZES = {"y": 4, "z": 8, "x": 4, "core": 2}
ROW = ("y", "z")
COL = ("x", "core")
VM = pltpu.VMEM
F32 = jnp.float32
BF16 = jnp.bfloat16
STEPS = (0, 1, 2, -1)


def from_ahead(value, axis, k):
    n = SIZES[axis]
    return lax.ppermute(value, axis, [((i + k) % n, i) for i in range(n)])


def to_ahead(value, axis, k):
    n = SIZES[axis]
    return lax.ppermute(value, axis, [(i, (i + k) % n) for i in range(n)])


def call(body, outs, smem, vmem, flops=0, scratch=(), limit=24):
    outs = [jax.ShapeDtypeStruct(s, d) for s, d in outs]
    return pl.pallas_call(
        body,
        out_shape=outs,
        in_specs=[pl.BlockSpec(memory_space=pltpu.SMEM)] * len(smem)
        + [pl.BlockSpec(memory_space=VM)] * len(vmem),
        out_specs=[pl.BlockSpec(memory_space=VM)] * len(outs),
        scratch_shapes=list(scratch),
        compiler_params=pltpu.CompilerParams(vmem_limit_bytes=limit * 2**20),
        cost_estimate=pl.CostEstimate(
            flops=flops,
            transcendentals=0,
            bytes_accessed=sum(v.size * v.dtype.itemsize for v in vmem)
            + sum(o.size * o.dtype.itemsize for o in outs),
        ),
    )(*smem, *vmem)


def tile_ref(ref, r, c):
    return ref.at[
        pl.ds(pl.multiple_of(r * TILE, TILE), TILE), pl.ds(pl.multiple_of(c * TILE, TILE), TILE)
    ]


def mask_body(rows, cols, count, w, out, flipped):
    out[...] = jnp.zeros_like(out)
    flipped[...] = jnp.zeros_like(flipped)

    @pl.loop(0, count[0])
    def _(k):
        tile = tile_ref(w, rows[k], cols[k])[...]
        tile_ref(out, rows[k], cols[k])[...] = tile
        tile_ref(flipped, cols[k], rows[k])[...] = tile.T


def zpos(pos, i, hi):
    return (pos[1] + i + 4 * hi + 8) % 8


def up_body(pos, *refs):
    a3, b3, w = refs[:4], refs[4:8], refs[8]
    keep, send1, send2, toks, acc = refs[9:]
    core = pos[3]
    cut = a3[0].shape[-1]
    back = pos[0] - pos[2] + 4
    for j in range(4):
        d = (j + back) % 4
        for i in range(4):

            @pl.loop(0, 2)
            def _(hi, i=i, j=j, d=d):
                at = zpos(pos, STEPS[i], hi)
                toks[d, at, :, :cut] = a3[i][j, hi]
                toks[d, at, :, cut:] = b3[j][i, hi]

    @pl.loop(0, 4)
    def _(d):
        part = jnp.dot(
            toks[d].reshape(-1, toks.shape[-1]), w[...], preferred_element_type=F32
        )
        acc[...] = part.reshape(acc.shape)
        keep[d] = acc[core]
        away = acc[1 - core].astype(BF16)
        half = send1.shape[2]
        send1[d] = away[:, :half]
        send2[d] = away[:, half:]


def collect(pos, mine, other, slots, sems):
    core = pos[3]
    copies = [
        pltpu.make_async_copy(g, slots(side), sems.at[s])
        for s, (side, g) in enumerate(((core, mine), (1 - core, other)))
    ]
    for c in copies:
        c.start()
    for c in copies:
        c.wait()


def back_first_body(pos, *refs):
    mine, other, w, total, grads, sems = refs
    collect(pos, mine, other, lambda side: grads.at[:, side], sems)

    @pl.loop(0, 4)
    def _(d):
        g = grads[d].reshape(-1, grads.shape[-1])
        part = jnp.dot(g, w[: g.shape[1]], preferred_element_type=F32)
        total[d] = part.reshape(total.shape[1:])


def back_second_body(pos, *refs):
    mine, other, w, total, first = refs[:5]
    a3, b3, grads = refs[5:9], refs[9:13], refs[13]
    acc, sems, first_sem = refs[14:]
    cut = first.shape[-1]
    kept = pltpu.make_async_copy(first, grads.at[:, :, :, pl.ds(0, cut)], first_sem)
    kept.start()
    collect(pos, mine, other, lambda side: grads.at[:, side, :, pl.ds(cut, cut)], sems)
    back = pos[0] - pos[2] + 4

    @pl.loop(0, 4)
    def _(j):
        d = (j + back) % 4
        g = grads[d, :, :, cut:].reshape(-1, cut)
        part = jnp.dot(g, w[cut:], preferred_element_type=F32)
        acc[j] = total[d] + part.reshape(total.shape[1:])

    kept.wait()
    cut = a3[0].shape[-1]
    for hi in range(2):
        for k in range(4):

            @pl.loop(0, 4)
            def _(j, k=k, hi=hi):
                piece = acc[j, zpos(pos, STEPS[k], hi), :, :cut]
                a3[k][j, hi] = piece.astype(a3[k].dtype)

            @pl.loop(0, 4)
            def _(i, k=k, hi=hi):
                piece = acc[k, zpos(pos, jnp.where(i == 3, -1, i), hi), :, cut:]
                b3[k][i, hi] = piece.astype(b3[k].dtype)


def add_body(cols, keep, recv, *out):
    for d in range(4):

        @pl.loop(0, keep.shape[1] // 16)
        def _(i, d=d):
            at = pl.ds(pl.multiple_of(i * 16, 16), 16)
            total = keep[d, at, cols] + recv[d, at].astype(F32)
            out[d][at] = total.astype(out[d].dtype)


def act_body(cols, own, r1, r2, r3, cot, hidden, grad_pre):
    @pl.loop(0, own.shape[0] // 16)
    def _(i):
        at = pl.ds(pl.multiple_of(i * 16, 16), 16)
        pre_act = own[at] + r1[at].astype(F32) + r2[at].astype(F32) + r3[at].astype(F32)
        gate = jax.nn.sigmoid(pre_act)
        hidden[at] = (pre_act * gate).astype(BF16)
        slope = gate * (1.0 + pre_act * (1.0 - gate))
        grad_pre[at] = (cot[at, cols].astype(F32) * slope).astype(BF16)


def wgrad_body(rows, cols, count, toks, grads, out, acc):
    acc[...] = jnp.zeros_like(acc)
    step = 512

    @pl.loop(0, 4)
    def _(d):
        t = toks[d].reshape(-1, toks.shape[-1])

        @pl.loop(0, acc.shape[1] // step)
        def _(k):
            at = pl.ds(pl.multiple_of(k * step, step), step)
            g = grads[d, :, :, at].reshape(-1, step)
            acc[:, at] += lax.dot_general(
                t, g, (((0,), (0,)), ((), ())), preferred_element_type=F32
            )

    out[...] = jnp.zeros_like(out)

    @pl.loop(0, count[0])
    def _(k):
        tile_ref(out, rows[k], cols[k])[...] = tile_ref(acc, rows[k], cols[k])[...].astype(BF16)


def gather_four(piece, axis):
    return [piece] + [from_ahead(piece, axis, k) for k in STEPS[1:]]


def ring_gather(piece, axis):
    ahead = from_ahead(piece, axis, 1)
    behind = from_ahead(piece, axis, -1)
    return [piece, ahead, from_ahead(ahead, axis, 1), behind]


def gather_tokens(tokens):
    pair = jnp.stack([tokens, from_ahead(tokens, "z", 4)])
    cut = tokens.shape[1] // 2
    a2 = gather_four(pair[:, :, :cut], "y")
    b2 = gather_four(pair[:, :, cut:], "z")
    a2, b2 = lax.optimization_barrier((a2, b2))
    return ring_gather(jnp.stack(a2), "z"), ring_gather(jnp.stack(b2), "y")


def partial_sums(keep, recv, cols):
    shape = (keep.shape[1], cols.stop - cols.start)
    body = functools.partial(add_body, cols)
    return call(body, [(shape, F32)] + [(shape, BF16)] * 3, [], [keep, recv])


def activation(own, sends, cot, cols):
    recvs = [to_ahead(s, "x", d + 1) for d, s in enumerate(sends)]
    body = functools.partial(act_body, cols)
    return call(body, [(own.shape, BF16)] * 2, [], [own] + recvs + [cot])


def gather_grads(grad_pre):
    mine = jnp.stack([grad_pre] + [from_ahead(grad_pre, "x", d) for d in range(1, 4)])
    return [mine, to_ahead(mine, "core", 1)]


def reduce_four(own, sends, axis):
    total = own
    for k, s in zip(STEPS[1:], sends):
        total = total + to_ahead(s.astype(BF16), axis, k).astype(F32)
    return total


def ring_reduce(own, ahead, far, behind, axis):
    through = to_ahead(far, axis, 1).astype(F32)
    total = own + to_ahead(behind, axis, -1).astype(F32)
    return total + to_ahead((ahead + through).astype(BF16), axis, 1).astype(F32)


def middle(a3, b3, wm, flipped, pos, cot):
    rows = a3[0].shape[2] * 4
    depth, width = wm.shape
    cut = width // 2
    flops = 8 * rows * depth * width
    keep, send1, send2, toks = call(
        up_body,
        [
            ((4, rows, width), F32),
            ((4, rows, cut), BF16),
            ((4, rows, cut), BF16),
            ((4, 8, rows // 4, depth), BF16),
        ],
        [pos],
        a3 + b3 + [wm],
        2 * flops,
        [VM((2, rows, width), F32)],
    )
    cols1, cols2 = slice(0, cut), slice(cut, width)
    own1, *sends1 = partial_sums(keep, to_ahead(send1, "core", 1), cols1)
    own2, *sends2 = partial_sums(keep, to_ahead(send2, "core", 1), cols2)
    hidden1, grad1 = activation(own1, sends1, cot, cols1)
    hidden2, grad2 = activation(own2, sends2, cot, cols2)
    hidden = jnp.concatenate([hidden1, hidden2], axis=1)
    parts1 = gather_grads(grad1)
    parts2 = gather_grads(grad2)
    g_shape = ((4, 2, rows, cut), BF16)
    sems = pltpu.SemaphoreType.DMA((2,))
    sums = (4, 8, rows // 4, depth)
    total, g1 = call(
        back_first_body, [(sums, F32), g_shape], [pos], parts1 + [flipped], flops, [sems]
    )
    shape = (4, 2, rows // 4, depth // 2)
    outs = [(shape, d) for d in (F32, F32, BF16, BF16)]
    *sends, grads = call(
        back_second_body,
        outs + outs + [((4, 2, rows, width), BF16)],
        [pos],
        parts2 + [flipped, total, g1],
        flops,
        [VM(sums, F32), sems, pltpu.SemaphoreType.DMA],
    )
    return hidden, sends, toks, grads


def reduce_inputs(sends, weight_grad):
    a2 = ring_reduce(*sends[:4], "z")
    b2 = ring_reduce(*sends[4:], "y")
    a2, b2, weight_grad = lax.optimization_barrier((a2, b2, weight_grad))
    a1 = reduce_four(a2[0], a2[1:], "y")
    b1 = reduce_four(b2[0], b2[1:], "z")
    both = jnp.concatenate([a1, b1], axis=-1)
    total = both[0] + to_ahead(both[1].astype(BF16), "z", 4).astype(F32)
    return total.astype(BF16), weight_grad


def on_device(tokens, weight, tile_rows, tile_cols, tile_count, hidden_cotangent):
    y, z, x, core = (lax.axis_index(a) for a in ("y", "z", "x", "core"))
    pos = jnp.stack([y, z, x, core]).astype(jnp.int32)
    row_blocks = weight.shape[0] // TILE
    col_blocks = weight.shape[1] // TILE
    rows = tile_rows.reshape(-1) - (x * 2 + core) * row_blocks
    cols = tile_cols.reshape(-1) - (y * 8 + z) * col_blocks
    count = tile_count.reshape(1)
    shapes = [(weight.shape, BF16), (weight.shape[::-1], BF16)]
    wm, flipped = call(mask_body, shapes, [rows, cols, count], [weight])
    a3, b3 = gather_tokens(tokens)
    hidden, sends, toks, grads = middle(a3, b3, wm, flipped, pos, hidden_cotangent)
    (weight_grad,) = call(
        wgrad_body,
        [(weight.shape, BF16)],
        [rows, cols, count],
        [toks, grads],
        2 * 1536 * weight.size,
        [VM(weight.shape, F32)],
    )
    input_grad, weight_grad = reduce_inputs(sends, weight_grad)
    return hidden, input_grad, weight_grad


def solution(mesh):
    split = Mesh(mesh.devices.reshape(4, 8, 4, 2), ("y", "z", "x", "core"))
    return jax.shard_map(
        on_device,
        mesh=split,
        in_specs=(
            P(ROW, COL),
            P(COL, ROW),
            P(ROW, COL, None),
            P(ROW, COL, None),
            P(ROW, COL),
            P(COL, ROW),
        ),
        out_specs=(P(COL, ROW), P(ROW, COL), P(COL, ROW)),
        check_vma=False,
    )
```

```python
import functools

import jax
import jax.numpy as jnp
from jax import lax
from jax.experimental import pallas as pl
from jax.experimental.pallas import tpu as pltpu
from jax.sharding import Mesh
from jax.sharding import PartitionSpec as P

TILE = 128
SIZES = {"y": 4, "z": 8, "x": 4, "core": 2}
ROW = ("y", "z")
COL = ("x", "core")
VM = pltpu.VMEM
F32 = jnp.float32
BF16 = jnp.bfloat16
STEPS = (0, 1, 2, -1)


def from_ahead(value, axis, k):
    n = SIZES[axis]
    return lax.ppermute(value, axis, [((i + k) % n, i) for i in range(n)])


def to_ahead(value, axis, k):
    n = SIZES[axis]
    return lax.ppermute(value, axis, [(i, (i + k) % n) for i in range(n)])


def call(body, outs, smem, vmem, flops=0, scratch=(), limit=24):
    outs = [jax.ShapeDtypeStruct(s, d) for s, d in outs]
    return pl.pallas_call(
        body,
        out_shape=outs,
        in_specs=[pl.BlockSpec(memory_space=pltpu.SMEM)] * len(smem)
        + [pl.BlockSpec(memory_space=VM)] * len(vmem),
        out_specs=[pl.BlockSpec(memory_space=VM)] * len(outs),
        scratch_shapes=list(scratch),
        compiler_params=pltpu.CompilerParams(vmem_limit_bytes=limit * 2**20),
        cost_estimate=pl.CostEstimate(
            flops=flops,
            transcendentals=0,
            bytes_accessed=sum(v.size * v.dtype.itemsize for v in vmem)
            + sum(o.size * o.dtype.itemsize for o in outs),
        ),
    )(*smem, *vmem)


def tile_ref(ref, r, c):
    return ref.at[
        pl.ds(pl.multiple_of(r * TILE, TILE), TILE), pl.ds(pl.multiple_of(c * TILE, TILE), TILE)
    ]


def mask_body(rows, cols, count, w, out, flipped):
    out[...] = jnp.zeros_like(out)
    flipped[...] = jnp.zeros_like(flipped)

    @pl.loop(0, count[0])
    def _(k):
        tile = tile_ref(w, rows[k], cols[k])[...]
        tile_ref(out, rows[k], cols[k])[...] = tile
        tile_ref(flipped, cols[k], rows[k])[...] = tile.T


def zpos(pos, i, hi):
    return (pos[1] + i + 4 * hi + 8) % 8


def up_body(pos, *refs):
    a3, b3, w = refs[:4], refs[4:8], refs[8]
    keep, send1, send2, toks, acc = refs[9:]
    core = pos[3]
    cut = a3[0].shape[-1]
    back = pos[0] - pos[2] + 4
    for j in range(4):
        d = (j + back) % 4
        for i in range(4):

            @pl.loop(0, 2)
            def _(hi, i=i, j=j, d=d):
                at = zpos(pos, STEPS[i], hi)
                toks[d, at, :, :cut] = a3[i][j, hi]
                toks[d, at, :, cut:] = b3[j][i, hi]

    @pl.loop(0, 4)
    def _(d):
        part = jnp.dot(
            toks[d].reshape(-1, toks.shape[-1]), w[...], preferred_element_type=F32
        )
        acc[...] = part.reshape(acc.shape)
        keep[d] = acc[core]
        away = acc[1 - core].astype(BF16)
        half = send1.shape[2]
        send1[d] = away[:, :half]
        send2[d] = away[:, half:]


def collect(pos, mine, other, slots, sems):
    core = pos[3]
    copies = [
        pltpu.make_async_copy(g, slots(side), sems.at[s])
        for s, (side, g) in enumerate(((core, mine), (1 - core, other)))
    ]
    for c in copies:
        c.start()
    for c in copies:
        c.wait()


def back_first_body(pos, *refs):
    mine, other, w, total, grads, sems = refs
    collect(pos, mine, other, lambda side: grads.at[:, side], sems)

    @pl.loop(0, 4)
    def _(d):
        g = grads[d].reshape(-1, grads.shape[-1])
        part = jnp.dot(g, w[: g.shape[1]], preferred_element_type=F32)
        total[d] = part.reshape(total.shape[1:])


def back_second_body(pos, *refs):
    mine, other, w, total, first = refs[:5]
    a3, b3, grads = refs[5:9], refs[9:13], refs[13]
    acc, sems, first_sem = refs[14:]
    cut = first.shape[-1]
    kept = pltpu.make_async_copy(first, grads.at[:, :, :, pl.ds(0, cut)], first_sem)
    kept.start()
    collect(pos, mine, other, lambda side: grads.at[:, side, :, pl.ds(cut, cut)], sems)
    back = pos[0] - pos[2] + 4

    @pl.loop(0, 4)
    def _(j):
        d = (j + back) % 4
        g = grads[d, :, :, cut:].reshape(-1, cut)
        part = jnp.dot(g, w[cut:], preferred_element_type=F32)
        acc[j] = total[d] + part.reshape(total.shape[1:])

    kept.wait()
    cut = a3[0].shape[-1]
    for hi in range(2):
        for k in range(4):

            @pl.loop(0, 4)
            def _(j, k=k, hi=hi):
                piece = acc[j, zpos(pos, STEPS[k], hi), :, :cut]
                a3[k][j, hi] = piece.astype(a3[k].dtype)

            @pl.loop(0, 4)
            def _(i, k=k, hi=hi):
                piece = acc[k, zpos(pos, jnp.where(i == 3, -1, i), hi), :, cut:]
                b3[k][i, hi] = piece.astype(b3[k].dtype)


def add_body(cols, way, keep, recv, *out):
    for k in range(4):
        d = k * way % 4

        @pl.loop(0, keep.shape[1] // 16)
        def _(i, d=d, k=k):
            at = pl.ds(pl.multiple_of(i * 16, 16), 16)
            total = keep[d, at, cols] + recv[d, at].astype(F32)
            out[k][at] = total.astype(out[k].dtype)


def act_body(cols, own, r1, r2, cot, hidden, grad_pre):
    @pl.loop(0, own.shape[0] // 16)
    def _(i):
        at = pl.ds(pl.multiple_of(i * 16, 16), 16)
        pre_act = own[at] + r1[at].astype(F32) + r2[at].astype(F32)
        gate = jax.nn.sigmoid(pre_act)
        hidden[at] = (pre_act * gate).astype(BF16)
        slope = gate * (1.0 + pre_act * (1.0 - gate))
        grad_pre[at] = (cot[at, cols].astype(F32) * slope).astype(BF16)


def wgrad_body(rows, cols, count, toks, grads, out, acc):
    acc[...] = jnp.zeros_like(acc)
    step = 512

    @pl.loop(0, 4)
    def _(d):
        t = toks[d].reshape(-1, toks.shape[-1])

        @pl.loop(0, acc.shape[1] // step)
        def _(k):
            at = pl.ds(pl.multiple_of(k * step, step), step)
            g = grads[d, :, :, at].reshape(-1, step)
            acc[:, at] += lax.dot_general(
                t, g, (((0,), (0,)), ((), ())), preferred_element_type=F32
            )

    out[...] = jnp.zeros_like(out)

    @pl.loop(0, count[0])
    def _(k):
        tile_ref(out, rows[k], cols[k])[...] = tile_ref(acc, rows[k], cols[k])[...].astype(BF16)


def gather_four(piece, axis):
    return [piece] + [from_ahead(piece, axis, k) for k in STEPS[1:]]


def ring_gather(piece, axis):
    ahead = from_ahead(piece, axis, 1)
    behind = from_ahead(piece, axis, -1)
    return [piece, ahead, from_ahead(ahead, axis, 1), behind]


def gather_tokens(tokens):
    pair = jnp.stack([tokens, from_ahead(tokens, "z", 4)])
    cut = tokens.shape[1] // 2
    a2 = gather_four(pair[:, :, :cut], "y")
    b2 = gather_four(pair[:, :, cut:], "z")
    a2, b2 = lax.optimization_barrier((a2, b2))
    return ring_gather(jnp.stack(a2), "z"), ring_gather(jnp.stack(b2), "y")


def partial_sums(keep, recv, cols, way):
    shape = (keep.shape[1], cols.stop - cols.start)
    body = functools.partial(add_body, cols, way)
    outs = [(shape, d) for d in (F32, F32, BF16, BF16)]
    return call(body, outs, [], [keep, recv])


def activation(own, near, far, other, cot, cols, way):
    behind = to_ahead(other, "x", -way)
    through = to_ahead(far, "x", way)
    near = to_ahead((near + through.astype(F32)).astype(BF16), "x", way)
    body = functools.partial(act_body, cols)
    return call(body, [(own.shape, BF16)] * 2, [], [own, near, behind, cot])


def gather_grads(grad_pre, way):
    near, other = from_ahead(grad_pre, "x", way), from_ahead(grad_pre, "x", -way)
    far = from_ahead(near, "x", way)
    mine = jnp.stack([grad_pre] + ([near, far, other] if way == 1 else [other, far, near]))
    return [mine, to_ahead(mine, "core", 1)]


def reduce_four(own, sends, axis):
    total = own
    for k, s in zip(STEPS[1:], sends):
        total = total + to_ahead(s.astype(BF16), axis, k).astype(F32)
    return total


def ring_reduce(own, ahead, far, behind, axis):
    through = to_ahead(far, axis, 1).astype(F32)
    total = own + to_ahead(behind, axis, -1).astype(F32)
    return total + to_ahead((ahead + through).astype(BF16), axis, 1).astype(F32)


def middle(a3, b3, wm, flipped, pos, cot):
    rows = a3[0].shape[2] * 4
    depth, width = wm.shape
    cut = width // 2
    flops = 8 * rows * depth * width
    keep, send1, send2, toks = call(
        up_body,
        [
            ((4, rows, width), F32),
            ((4, rows, cut), BF16),
            ((4, rows, cut), BF16),
            ((4, 8, rows // 4, depth), BF16),
        ],
        [pos],
        a3 + b3 + [wm],
        2 * flops,
        [VM((2, rows, width), F32)],
    )
    cols1, cols2 = slice(0, cut), slice(cut, width)
    sums1 = partial_sums(keep, to_ahead(send1, "core", 1), cols1, 1)
    sums2 = partial_sums(keep, to_ahead(send2, "core", 1), cols2, -1)
    hidden1, grad1 = activation(*sums1, cot, cols1, 1)
    hidden2, grad2 = activation(*sums2, cot, cols2, -1)
    hidden = jnp.concatenate([hidden1, hidden2], axis=1)
    parts1 = gather_grads(grad1, -1)
    parts2 = gather_grads(grad2, 1)
    g_shape = ((4, 2, rows, cut), BF16)
    sems = pltpu.SemaphoreType.DMA((2,))
    sums = (4, 8, rows // 4, depth)
    total, g1 = call(
        back_first_body, [(sums, F32), g_shape], [pos], parts1 + [flipped], flops, [sems]
    )
    shape = (4, 2, rows // 4, depth // 2)
    outs = [(shape, d) for d in (F32, F32, BF16, BF16)]
    *sends, grads = call(
        back_second_body,
        outs + outs + [((4, 2, rows, width), BF16)],
        [pos],
        parts2 + [flipped, total, g1],
        flops,
        [VM(sums, F32), sems, pltpu.SemaphoreType.DMA],
    )
    return hidden, sends, toks, grads


def reduce_inputs(sends, weight_grad):
    a2 = ring_reduce(*sends[:4], "z")
    b2 = ring_reduce(*sends[4:], "y")
    a2, b2, weight_grad = lax.optimization_barrier((a2, b2, weight_grad))
    a1 = reduce_four(a2[0], a2[1:], "y")
    b1 = reduce_four(b2[0], b2[1:], "z")
    both = jnp.concatenate([a1, b1], axis=-1)
    total = both[0] + to_ahead(both[1].astype(BF16), "z", 4).astype(F32)
    return total.astype(BF16), weight_grad


def on_device(tokens, weight, tile_rows, tile_cols, tile_count, hidden_cotangent):
    y, z, x, core = (lax.axis_index(a) for a in ("y", "z", "x", "core"))
    pos = jnp.stack([y, z, x, core]).astype(jnp.int32)
    row_blocks = weight.shape[0] // TILE
    col_blocks = weight.shape[1] // TILE
    rows = tile_rows.reshape(-1) - (x * 2 + core) * row_blocks
    cols = tile_cols.reshape(-1) - (y * 8 + z) * col_blocks
    count = tile_count.reshape(1)
    shapes = [(weight.shape, BF16), (weight.shape[::-1], BF16)]
    wm, flipped = call(mask_body, shapes, [rows, cols, count], [weight])
    a3, b3 = gather_tokens(tokens)
    hidden, sends, toks, grads = middle(a3, b3, wm, flipped, pos, hidden_cotangent)
    (weight_grad,) = call(
        wgrad_body,
        [(weight.shape, BF16)],
        [rows, cols, count],
        [toks, grads],
        2 * 1536 * weight.size,
        [VM(weight.shape, F32)],
    )
    input_grad, weight_grad = reduce_inputs(sends, weight_grad)
    return hidden, input_grad, weight_grad


def solution(mesh):
    split = Mesh(mesh.devices.reshape(4, 8, 4, 2), ("y", "z", "x", "core"))
    return jax.shard_map(
        on_device,
        mesh=split,
        in_specs=(
            P(ROW, COL),
            P(COL, ROW),
            P(ROW, COL, None),
            P(ROW, COL, None),
            P(ROW, COL),
            P(COL, ROW),
        ),
        out_specs=(P(COL, ROW), P(ROW, COL), P(COL, ROW)),
        check_vma=False,
    )
```

```python
import functools

import jax
import jax.numpy as jnp
from jax import lax
from jax.experimental import pallas as pl
from jax.experimental.pallas import tpu as pltpu
from jax.sharding import Mesh
from jax.sharding import PartitionSpec as P

TILE = 128
SIZES = {"y": 4, "z": 8, "x": 4, "core": 2}
ROW = ("y", "z")
COL = ("x", "core")
VM = pltpu.VMEM
F32 = jnp.float32
BF16 = jnp.bfloat16
STEPS = (0, 1, 2, -1)


def from_ahead(value, axis, k):
    n = SIZES[axis]
    return lax.ppermute(value, axis, [((i + k) % n, i) for i in range(n)])


def to_ahead(value, axis, k):
    n = SIZES[axis]
    return lax.ppermute(value, axis, [(i, (i + k) % n) for i in range(n)])


def ring_pairs(axis, k):
    n = SIZES[axis]
    return [(i * 2 + c, (i + (k if c == 0 else -k)) % n * 2 + c) for i in range(n) for c in range(2)]


def ring_from(value, axis, k):
    return lax.ppermute(value, (axis, "core"), [(b, a) for a, b in ring_pairs(axis, k)])


def ring_to(value, axis, k):
    return lax.ppermute(value, (axis, "core"), ring_pairs(axis, k))


def call(body, outs, smem, vmem, flops=0, scratch=(), limit=24):
    outs = [jax.ShapeDtypeStruct(s, d) for s, d in outs]
    return pl.pallas_call(
        body,
        out_shape=outs,
        in_specs=[pl.BlockSpec(memory_space=pltpu.SMEM)] * len(smem)
        + [pl.BlockSpec(memory_space=VM)] * len(vmem),
        out_specs=[pl.BlockSpec(memory_space=VM)] * len(outs),
        scratch_shapes=list(scratch),
        compiler_params=pltpu.CompilerParams(vmem_limit_bytes=limit * 2**20),
        cost_estimate=pl.CostEstimate(
            flops=flops,
            transcendentals=0,
            bytes_accessed=sum(v.size * v.dtype.itemsize for v in vmem)
            + sum(o.size * o.dtype.itemsize for o in outs),
        ),
    )(*smem, *vmem)


def tile_ref(ref, r, c):
    return ref.at[
        pl.ds(pl.multiple_of(r * TILE, TILE), TILE), pl.ds(pl.multiple_of(c * TILE, TILE), TILE)
    ]


def mask_body(rows, cols, count, w, out, flipped):
    out[...] = jnp.zeros_like(out)
    flipped[...] = jnp.zeros_like(flipped)

    @pl.loop(0, count[0])
    def _(k):
        tile = tile_ref(w, rows[k], cols[k])[...]
        tile_ref(out, rows[k], cols[k])[...] = tile
        tile_ref(flipped, cols[k], rows[k])[...] = tile.T


def zpos(pos, i, hi):
    return (pos[1] + i + 4 * hi + 8) % 8


def up_body(pos, *refs):
    a3, b3, w = refs[:4], refs[4:8], refs[8]
    keep, send1, send2, toks, acc = refs[9:]
    core = pos[3]
    cut = a3[0].shape[-1]
    way = 1 - 2 * core
    back = pos[0] - pos[2] + 4
    for j in range(4):
        d = (j + back) % 4
        for i in range(4):

            @pl.loop(0, 2)
            def _(hi, i=i, j=j, d=d):
                low = zpos(pos, way * STEPS[i], hi)
                high = zpos(pos, STEPS[i], hi)
                toks[d, low, :, :cut] = a3[i][j, hi]
                toks[(j * way + back + 4) % 4, high, :, cut:] = b3[j][i, hi]

    @pl.loop(0, 4)
    def _(d):
        part = jnp.dot(
            toks[d].reshape(-1, toks.shape[-1]), w[...], preferred_element_type=F32
        )
        acc[...] = part.reshape(acc.shape)
        keep[d] = acc[core]
        away = acc[1 - core].astype(BF16)
        half = send1.shape[2]
        send1[d] = away[:, :half]
        send2[d] = away[:, half:]


def collect(pos, mine, other, slots, sems):
    core = pos[3]
    copies = [
        pltpu.make_async_copy(g, slots(side), sems.at[s])
        for s, (side, g) in enumerate(((core, mine), (1 - core, other)))
    ]
    for c in copies:
        c.start()
    for c in copies:
        c.wait()


def back_first_body(pos, *refs):
    mine, other, w, total, grads, sems = refs
    collect(pos, mine, other, lambda side: grads.at[:, side], sems)

    @pl.loop(0, 4)
    def _(d):
        g = grads[d].reshape(-1, grads.shape[-1])
        part = jnp.dot(g, w[: g.shape[1]], preferred_element_type=F32)
        total[d] = part.reshape(total.shape[1:])


def back_second_body(pos, *refs):
    mine, other, w, total, first = refs[:5]
    a3, b3, grads = refs[5:9], refs[9:13], refs[13]
    acc, sems, first_sem = refs[14:]
    cut = first.shape[-1]
    kept = pltpu.make_async_copy(first, grads.at[:, :, :, pl.ds(0, cut)], first_sem)
    kept.start()
    collect(pos, mine, other, lambda side: grads.at[:, side, :, pl.ds(cut, cut)], sems)
    way = 1 - 2 * pos[3]
    back = pos[0] - pos[2] + 4

    @pl.loop(0, 4)
    def _(j):
        d = (j + back) % 4
        g = grads[d, :, :, cut:].reshape(-1, cut)
        part = jnp.dot(g, w[cut:], preferred_element_type=F32)
        acc[j] = total[d] + part.reshape(total.shape[1:])

    kept.wait()
    cut = a3[0].shape[-1]
    for hi in range(2):
        for k in range(4):

            @pl.loop(0, 4)
            def _(j, k=k, hi=hi):
                piece = acc[j, zpos(pos, way * STEPS[k], hi), :, :cut]
                a3[k][j, hi] = piece.astype(a3[k].dtype)

            @pl.loop(0, 4)
            def _(i, k=k, hi=hi):
                j = (k * way + 4) % 4
                piece = acc[j, zpos(pos, jnp.where(i == 3, -1, i), hi), :, cut:]
                b3[k][i, hi] = piece.astype(b3[k].dtype)


def add_body(cols, way, keep, recv, *out):
    for k in range(4):
        d = k * way % 4

        @pl.loop(0, keep.shape[1] // 16)
        def _(i, d=d, k=k):
            at = pl.ds(pl.multiple_of(i * 16, 16), 16)
            total = keep[d, at, cols] + recv[d, at].astype(F32)
            out[k][at] = total.astype(out[k].dtype)


def act_body(cols, own, r1, r2, cot, hidden, grad_pre):
    @pl.loop(0, own.shape[0] // 16)
    def _(i):
        at = pl.ds(pl.multiple_of(i * 16, 16), 16)
        pre_act = own[at] + r1[at].astype(F32) + r2[at].astype(F32)
        gate = jax.nn.sigmoid(pre_act)
        hidden[at] = (pre_act * gate).astype(BF16)
        slope = gate * (1.0 + pre_act * (1.0 - gate))
        grad_pre[at] = (cot[at, cols].astype(F32) * slope).astype(BF16)


def wgrad_body(rows, cols, count, toks, grads, out, acc):
    acc[...] = jnp.zeros_like(acc)
    step = 512

    @pl.loop(0, 4)
    def _(d):
        t = toks[d].reshape(-1, toks.shape[-1])

        @pl.loop(0, acc.shape[1] // step)
        def _(k):
            at = pl.ds(pl.multiple_of(k * step, step), step)
            g = grads[d, :, :, at].reshape(-1, step)
            acc[:, at] += lax.dot_general(
                t, g, (((0,), (0,)), ((), ())), preferred_element_type=F32
            )

    out[...] = jnp.zeros_like(out)

    @pl.loop(0, count[0])
    def _(k):
        tile_ref(out, rows[k], cols[k])[...] = tile_ref(acc, rows[k], cols[k])[...].astype(BF16)


def gather_four(piece, axis):
    return [piece] + [from_ahead(piece, axis, k) for k in STEPS[1:]]


def ring_gather(piece, axis):
    ahead = ring_from(piece, axis, 1)
    behind = ring_from(piece, axis, -1)
    return [piece, ahead, ring_from(ahead, axis, 1), behind]


def gather_tokens(tokens):
    pair = jnp.stack([tokens, from_ahead(tokens, "z", 4)])
    cut = tokens.shape[1] // 2
    a2 = gather_four(pair[:, :, :cut], "y")
    b2 = gather_four(pair[:, :, cut:], "z")
    a2, b2 = lax.optimization_barrier((a2, b2))
    return ring_gather(jnp.stack(a2), "z"), ring_gather(jnp.stack(b2), "y")


def partial_sums(keep, recv, cols, way):
    shape = (keep.shape[1], cols.stop - cols.start)
    body = functools.partial(add_body, cols, way)
    outs = [(shape, d) for d in (F32, F32, BF16, BF16)]
    return call(body, outs, [], [keep, recv])


def activation(own, near, far, other, cot, cols, way):
    behind = to_ahead(other, "x", -way)
    through = to_ahead(far, "x", way)
    near = to_ahead((near + through.astype(F32)).astype(BF16), "x", way)
    body = functools.partial(act_body, cols)
    return call(body, [(own.shape, BF16)] * 2, [], [own, near, behind, cot])


def gather_grads(grad_pre, way):
    near, other = from_ahead(grad_pre, "x", way), from_ahead(grad_pre, "x", -way)
    far = from_ahead(near, "x", way)
    mine = jnp.stack([grad_pre] + ([near, far, other] if way == 1 else [other, far, near]))
    return [mine, to_ahead(mine, "core", 1)]


def reduce_four(own, sends, axis):
    total = own
    for k, s in zip(STEPS[1:], sends):
        total = total + to_ahead(s.astype(BF16), axis, k).astype(F32)
    return total


def ring_reduce(own, ahead, far, behind, axis):
    through = ring_to(far, axis, 1).astype(F32)
    total = own + ring_to(behind, axis, -1).astype(F32)
    return total + ring_to((ahead + through).astype(BF16), axis, 1).astype(F32)


def middle(a3, b3, wm, flipped, pos, cot):
    rows = a3[0].shape[2] * 4
    depth, width = wm.shape
    cut = width // 2
    flops = 8 * rows * depth * width
    keep, send1, send2, toks = call(
        up_body,
        [
            ((4, rows, width), F32),
            ((4, rows, cut), BF16),
            ((4, rows, cut), BF16),
            ((4, 8, rows // 4, depth), BF16),
        ],
        [pos],
        a3 + b3 + [wm],
        2 * flops,
        [VM((2, rows, width), F32)],
    )
    cols1, cols2 = slice(0, cut), slice(cut, width)
    sums1 = partial_sums(keep, to_ahead(send1, "core", 1), cols1, 1)
    sums2 = partial_sums(keep, to_ahead(send2, "core", 1), cols2, -1)
    hidden1, grad1 = activation(*sums1, cot, cols1, 1)
    hidden2, grad2 = activation(*sums2, cot, cols2, -1)
    hidden = jnp.concatenate([hidden1, hidden2], axis=1)
    parts1 = gather_grads(grad1, -1)
    parts2 = gather_grads(grad2, 1)
    g_shape = ((4, 2, rows, cut), BF16)
    sems = pltpu.SemaphoreType.DMA((2,))
    sums = (4, 8, rows // 4, depth)
    total, g1 = call(
        back_first_body, [(sums, F32), g_shape], [pos], parts1 + [flipped], flops, [sems]
    )
    shape = (4, 2, rows // 4, depth // 2)
    outs = [(shape, d) for d in (F32, F32, BF16, BF16)]
    *sends, grads = call(
        back_second_body,
        outs + outs + [((4, 2, rows, width), BF16)],
        [pos],
        parts2 + [flipped, total, g1],
        flops,
        [VM(sums, F32), sems, pltpu.SemaphoreType.DMA],
    )
    return hidden, sends, toks, grads


def reduce_inputs(sends, weight_grad):
    a2 = ring_reduce(*sends[:4], "z")
    b2 = ring_reduce(*sends[4:], "y")
    a2, b2, weight_grad = lax.optimization_barrier((a2, b2, weight_grad))
    a1 = reduce_four(a2[0], a2[1:], "y")
    b1 = reduce_four(b2[0], b2[1:], "z")
    both = jnp.concatenate([a1, b1], axis=-1)
    total = both[0] + to_ahead(both[1].astype(BF16), "z", 4).astype(F32)
    return total.astype(BF16), weight_grad


def on_device(tokens, weight, tile_rows, tile_cols, tile_count, hidden_cotangent):
    y, z, x, core = (lax.axis_index(a) for a in ("y", "z", "x", "core"))
    pos = jnp.stack([y, z, x, core]).astype(jnp.int32)
    row_blocks = weight.shape[0] // TILE
    col_blocks = weight.shape[1] // TILE
    rows = tile_rows.reshape(-1) - (x * 2 + core) * row_blocks
    cols = tile_cols.reshape(-1) - (y * 8 + z) * col_blocks
    count = tile_count.reshape(1)
    shapes = [(weight.shape, BF16), (weight.shape[::-1], BF16)]
    wm, flipped = call(mask_body, shapes, [rows, cols, count], [weight])
    a3, b3 = gather_tokens(tokens)
    hidden, sends, toks, grads = middle(a3, b3, wm, flipped, pos, hidden_cotangent)
    (weight_grad,) = call(
        wgrad_body,
        [(weight.shape, BF16)],
        [rows, cols, count],
        [toks, grads],
        2 * 1536 * weight.size,
        [VM(weight.shape, F32)],
    )
    input_grad, weight_grad = reduce_inputs(sends, weight_grad)
    return hidden, input_grad, weight_grad


def solution(mesh):
    split = Mesh(mesh.devices.reshape(4, 8, 4, 2), ("y", "z", "x", "core"))
    return jax.shard_map(
        on_device,
        mesh=split,
        in_specs=(
            P(ROW, COL),
            P(COL, ROW),
            P(ROW, COL, None),
            P(ROW, COL, None),
            P(ROW, COL),
            P(COL, ROW),
        ),
        out_specs=(P(COL, ROW), P(ROW, COL), P(COL, ROW)),
        check_vma=False,
    )
```

```python
import functools

import jax
import jax.numpy as jnp
from jax import lax
from jax.experimental import pallas as pl
from jax.experimental.pallas import tpu as pltpu
from jax.sharding import Mesh
from jax.sharding import PartitionSpec as P

TILE = 128
SIZES = {"y": 4, "z": 8, "x": 4, "core": 2}
ROW = ("y", "z")
COL = ("x", "core")
VM = pltpu.VMEM
F32 = jnp.float32
BF16 = jnp.bfloat16
STEPS = (0, 1, 2, -1)


def from_ahead(value, axis, k):
    n = SIZES[axis]
    return lax.ppermute(value, axis, [((i + k) % n, i) for i in range(n)])


def to_ahead(value, axis, k):
    n = SIZES[axis]
    return lax.ppermute(value, axis, [(i, (i + k) % n) for i in range(n)])


def ring_pairs(axis, k):
    n = SIZES[axis]
    return [(i * 2 + c, (i + (k if c == 0 else -k)) % n * 2 + c) for i in range(n) for c in range(2)]


def ring_from(value, axis, k):
    return lax.ppermute(value, (axis, "core"), [(b, a) for a, b in ring_pairs(axis, k)])


def ring_to(value, axis, k):
    return lax.ppermute(value, (axis, "core"), ring_pairs(axis, k))


def call(body, outs, smem, vmem, flops=0, scratch=(), limit=24):
    outs = [jax.ShapeDtypeStruct(s, d) for s, d in outs]
    return pl.pallas_call(
        body,
        out_shape=outs,
        in_specs=[pl.BlockSpec(memory_space=pltpu.SMEM)] * len(smem)
        + [pl.BlockSpec(memory_space=VM)] * len(vmem),
        out_specs=[pl.BlockSpec(memory_space=VM)] * len(outs),
        scratch_shapes=list(scratch),
        compiler_params=pltpu.CompilerParams(vmem_limit_bytes=limit * 2**20),
        cost_estimate=pl.CostEstimate(
            flops=flops,
            transcendentals=0,
            bytes_accessed=sum(v.size * v.dtype.itemsize for v in vmem)
            + sum(o.size * o.dtype.itemsize for o in outs),
        ),
    )(*smem, *vmem)


def tile_ref(ref, r, c):
    return ref.at[
        pl.ds(pl.multiple_of(r * TILE, TILE), TILE), pl.ds(pl.multiple_of(c * TILE, TILE), TILE)
    ]


def mask_body(rows, cols, count, w, out, flipped):
    out[...] = jnp.zeros_like(out)
    flipped[...] = jnp.zeros_like(flipped)

    @pl.loop(0, count[0])
    def _(k):
        tile = tile_ref(w, rows[k], cols[k])[...]
        tile_ref(out, rows[k], cols[k])[...] = tile
        tile_ref(flipped, cols[k], rows[k])[...] = tile.T


def zpos(pos, i, hi):
    return (pos[1] + i + 4 * hi + 8) % 8


def up_body(pos, *refs):
    a3, b3, w = refs[:4], refs[4:8], refs[8]
    keep, send1, send2, toks, acc = refs[9:]
    core = pos[3]
    cut = a3[0].shape[-1]
    way = 1 - 2 * core
    back = pos[0] - pos[2] + 4
    for j in range(4):
        d = (j + back) % 4
        for i in range(4):

            @pl.loop(0, 2)
            def _(hi, i=i, j=j, d=d):
                low = zpos(pos, way * STEPS[i], hi)
                high = zpos(pos, STEPS[i], hi)
                toks[d, low, :, :cut] = a3[i][j, hi]
                toks[(j * way + back + 4) % 4, high, :, cut:] = b3[j][i, hi]

    @pl.loop(0, 4)
    def _(d):
        part = jnp.dot(
            toks[d].reshape(-1, toks.shape[-1]), w[...], preferred_element_type=F32
        )
        acc[...] = part.reshape(acc.shape)
        keep[d] = acc[core]
        away = acc[1 - core].astype(BF16)
        half = send1.shape[2]
        send1[d] = away[:, :half]
        send2[d] = away[:, half:]


def collect(pos, mine, other, slots, sems):
    core = pos[3]
    copies = [
        pltpu.make_async_copy(g, slots(side), sems.at[s])
        for s, (side, g) in enumerate(((core, mine), (1 - core, other)))
    ]
    for c in copies:
        c.start()
    for c in copies:
        c.wait()


def back_first_body(pos, *refs):
    mine, other, w, total, grads, sems = refs
    collect(pos, mine, other, lambda side: grads.at[:, side], sems)

    @pl.loop(0, 4)
    def _(d):
        g = grads[d].reshape(-1, grads.shape[-1])
        part = jnp.dot(g, w[: g.shape[1]], preferred_element_type=F32)
        total[d] = part.reshape(total.shape[1:])


def back_second_body(pos, *refs):
    mine, other, w, total, first = refs[:5]
    a3, b3, grads = refs[5:9], refs[9:13], refs[13]
    acc, sems, first_sem = refs[14:]
    cut = first.shape[-1]
    kept = pltpu.make_async_copy(first, grads.at[:, :, :, pl.ds(0, cut)], first_sem)
    kept.start()
    collect(pos, mine, other, lambda side: grads.at[:, side, :, pl.ds(cut, cut)], sems)
    way = 1 - 2 * pos[3]
    back = pos[0] - pos[2] + 4

    @pl.loop(0, 4)
    def _(j):
        d = (j + back) % 4
        g = grads[d, :, :, cut:].reshape(-1, cut)
        part = jnp.dot(g, w[cut:], preferred_element_type=F32)
        acc[j] = total[d] + part.reshape(total.shape[1:])

    kept.wait()
    cut = a3[0].shape[-1]
    for hi in range(2):
        for k in range(4):

            @pl.loop(0, 4)
            def _(j, k=k, hi=hi):
                piece = acc[j, zpos(pos, way * STEPS[k], hi), :, :cut]
                a3[k][j, hi] = piece.astype(a3[k].dtype)

            @pl.loop(0, 4)
            def _(i, k=k, hi=hi):
                j = (k * way + 4) % 4
                piece = acc[j, zpos(pos, jnp.where(i == 3, -1, i), hi), :, cut:]
                b3[k][i, hi] = piece.astype(b3[k].dtype)


def add_body(cols, way, keep, recv, *out):
    for k in range(4):
        d = k * way % 4

        @pl.loop(0, keep.shape[1] // 16)
        def _(i, d=d, k=k):
            at = pl.ds(pl.multiple_of(i * 16, 16), 16)
            total = keep[d, at, cols] + recv[d, at].astype(F32)
            out[k][at] = total.astype(out[k].dtype)


def act_body(cols, own, r1, r2, cot, hidden, grad_pre):
    @pl.loop(0, own.shape[0] // 16)
    def _(i):
        at = pl.ds(pl.multiple_of(i * 16, 16), 16)
        pre_act = own[at] + r1[at].astype(F32) + r2[at].astype(F32)
        gate = jax.nn.sigmoid(pre_act)
        hidden[at] = (pre_act * gate).astype(BF16)
        slope = gate * (1.0 + pre_act * (1.0 - gate))
        grad_pre[at] = (cot[at, cols].astype(F32) * slope).astype(BF16)


def wgrad_body(rows, cols, count, toks, grads, out, acc):
    acc[...] = jnp.zeros_like(acc)
    step = 512

    @pl.loop(0, 4)
    def _(d):
        t = toks[d].reshape(-1, toks.shape[-1])

        @pl.loop(0, acc.shape[1] // step)
        def _(k):
            at = pl.ds(pl.multiple_of(k * step, step), step)
            g = grads[d, :, :, at].reshape(-1, step)
            acc[:, at] += lax.dot_general(
                t, g, (((0,), (0,)), ((), ())), preferred_element_type=F32
            )

    out[...] = jnp.zeros_like(out)

    @pl.loop(0, count[0])
    def _(k):
        tile_ref(out, rows[k], cols[k])[...] = tile_ref(acc, rows[k], cols[k])[...].astype(BF16)


def gather_four(piece, axis):
    return [piece] + [from_ahead(piece, axis, k) for k in STEPS[1:]]


def ring_gather(piece, axis):
    ahead = ring_from(piece, axis, 1)
    behind = ring_from(piece, axis, -1)
    return [piece, ahead, ring_from(ahead, axis, 1), behind]


def gather_tokens(tokens):
    pair = jnp.stack([tokens, from_ahead(tokens, "z", 4)])
    cut = tokens.shape[1] // 2
    a2 = gather_four(pair[:, :, :cut], "y")
    b2 = gather_four(pair[:, :, cut:], "z")
    a2, b2 = lax.optimization_barrier((a2, b2))
    return ring_gather(jnp.stack(a2), "z"), ring_gather(jnp.stack(b2), "y")


def partial_sums(keep, recv, cols, way):
    shape = (keep.shape[1], cols.stop - cols.start)
    body = functools.partial(add_body, cols, way)
    outs = [(shape, d) for d in (F32, F32, BF16, BF16)]
    return call(body, outs, [], [keep, recv])


def activation(own, near, far, other, cot, cols, way):
    behind = to_ahead(other, "x", -way)
    through = to_ahead(far, "x", way)
    near = to_ahead((near + through.astype(F32)).astype(BF16), "x", way)
    body = functools.partial(act_body, cols)
    return call(body, [(own.shape, BF16)] * 2, [], [own, near, behind, cot])


def gather_grads(grad_pre, way):
    near, other = from_ahead(grad_pre, "x", way), from_ahead(grad_pre, "x", -way)
    far = from_ahead(near, "x", way)
    mine = jnp.stack([grad_pre] + ([near, far, other] if way == 1 else [other, far, near]))
    return [mine, to_ahead(mine, "core", 1)]


def reduce_four(own, sends, axis):
    total = own
    for k, s in zip(STEPS[1:], sends):
        total = total + to_ahead(s.astype(BF16), axis, k).astype(F32)
    return total


def ring_reduce(own, ahead, far, behind, axis):
    through = ring_to(far, axis, 1).astype(F32)
    total = own + ring_to(behind, axis, -1).astype(F32)
    return total + ring_to((ahead + through).astype(BF16), axis, 1).astype(F32)


def middle(a3, b3, wm, flipped, pos, cot):
    rows = a3[0].shape[2] * 4
    depth, width = wm.shape
    cut = width // 2
    flops = 8 * rows * depth * width
    keep, send1, send2, toks = call(
        up_body,
        [
            ((4, rows, width), F32),
            ((4, rows, cut), BF16),
            ((4, rows, cut), BF16),
            ((4, 8, rows // 4, depth), BF16),
        ],
        [pos],
        a3 + b3 + [wm],
        2 * flops,
        [VM((2, rows, width), F32)],
    )
    cols1, cols2 = slice(0, cut), slice(cut, width)
    sums1 = partial_sums(keep, to_ahead(send1, "core", 1), cols1, 1)
    sums2 = partial_sums(keep, to_ahead(send2, "core", 1), cols2, -1)
    hidden1, grad1 = activation(*sums1, cot, cols1, 1)
    hidden2, grad2 = activation(*sums2, cot, cols2, -1)
    hidden = jnp.concatenate([hidden1, hidden2], axis=1)
    parts1 = gather_grads(grad1, -1)
    parts2 = gather_grads(grad2, 1)
    g_shape = ((4, 2, rows, cut), BF16)
    sems = pltpu.SemaphoreType.DMA((2,))
    sums = (4, 8, rows // 4, depth)
    total, g1 = call(
        back_first_body, [(sums, F32), g_shape], [pos], parts1 + [flipped], flops, [sems]
    )
    shape = (4, 2, rows // 4, depth // 2)
    outs = [(shape, d) for d in (F32, F32, BF16, BF16)]
    *sends, grads = call(
        back_second_body,
        outs + outs + [((4, 2, rows, width), BF16)],
        [pos],
        parts2 + [flipped, total, g1],
        flops,
        [VM(sums, F32), sems, pltpu.SemaphoreType.DMA],
    )
    return hidden, sends, toks, grads


def reduce_inputs(sends, weight_grad):
    a2 = ring_reduce(*sends[:4], "z")
    b2 = ring_reduce(*sends[4:], "y")
    a2, b2 = lax.optimization_barrier((a2, b2))
    a1 = reduce_four(a2[0], a2[1:], "y")
    b1 = reduce_four(b2[0], b2[1:], "z")
    both = jnp.concatenate([a1, b1], axis=-1)
    total = both[0] + to_ahead(both[1].astype(BF16), "z", 4).astype(F32)
    return total.astype(BF16), weight_grad


def on_device(tokens, weight, tile_rows, tile_cols, tile_count, hidden_cotangent):
    y, z, x, core = (lax.axis_index(a) for a in ("y", "z", "x", "core"))
    pos = jnp.stack([y, z, x, core]).astype(jnp.int32)
    row_blocks = weight.shape[0] // TILE
    col_blocks = weight.shape[1] // TILE
    rows = tile_rows.reshape(-1) - (x * 2 + core) * row_blocks
    cols = tile_cols.reshape(-1) - (y * 8 + z) * col_blocks
    count = tile_count.reshape(1)
    shapes = [(weight.shape, BF16), (weight.shape[::-1], BF16)]
    wm, flipped = call(mask_body, shapes, [rows, cols, count], [weight])
    a3, b3 = gather_tokens(tokens)
    hidden, sends, toks, grads = middle(a3, b3, wm, flipped, pos, hidden_cotangent)
    (weight_grad,) = call(
        wgrad_body,
        [(weight.shape, BF16)],
        [rows, cols, count],
        [toks, grads],
        2 * 1536 * weight.size,
        [VM(weight.shape, F32)],
    )
    input_grad, weight_grad = reduce_inputs(sends, weight_grad)
    return hidden, input_grad, weight_grad


def solution(mesh):
    split = Mesh(mesh.devices.reshape(4, 8, 4, 2), ("y", "z", "x", "core"))
    return jax.shard_map(
        on_device,
        mesh=split,
        in_specs=(
            P(ROW, COL),
            P(COL, ROW),
            P(ROW, COL, None),
            P(ROW, COL, None),
            P(ROW, COL),
            P(COL, ROW),
        ),
        out_specs=(P(COL, ROW), P(ROW, COL), P(COL, ROW)),
        check_vma=False,
    )
```
